256 devices in a mesh: hid: 32 (over z, y), wid: 8 (over x, core).
Axes of the slice: x: 4, y: 4, z: 8, core: 2. Of those that a mesh axis runs over, the one named last changes fastest.
Arguments:
- inputs: bfloat16 [256, 12288], P(None, 'wid'), may hold values from -6 to 6
- gate_pre: bfloat16 [256, 32768], P(None, 'hid'), may hold values from -8 to 8
- up_pre: bfloat16 [256, 32768], P(None, 'hid'), may hold values from -6 to 6
- out_grad: bfloat16 [256, 12288], P(None, 'wid'), may hold values from -6 to 6
- gate_codes: int32 [6144, 32768], P('wid', 'hid'), may hold values from 0 to 255
- up_codes: int32 [6144, 32768], P('wid', 'hid'), may hold values from 0 to 255
- down_codes: int32 [16384, 12288], P('hid', 'wid'), may hold values from 0 to 255
- gate_scale: float32 [96, 32768], P('wid', 'hid'), may hold values from 0.0010825318 to 0.0027063293
- up_scale: float32 [96, 32768], P('wid', 'hid'), may hold values from 0.0010825318 to 0.0027063293
- down_scale: float32 [256, 12288], P('hid', 'wid'), may hold values from 0.0006629126 to 0.0016572815
Outputs:
- input_grad: bfloat16 [256, 12288], P('hid', 'wid')
- gate_log_grad: float32 [96, 32768], P('wid', 'hid')
- up_log_grad: float32 [96, 32768], P('wid', 'hid')
- down_log_grad: float32 [256, 12288], P('hid', 'wid')
The draws below stay inside these ranges and needn't reach their ends.
Inputs may be any that keep to these rules, and one draw needn't show every extreme that they name: `gate_codes`: each word holds two independent four-bit codes. `up_codes`: each word holds two independent four-bit codes. `down_codes`: each word holds two independent four-bit codes.
All inputs are finite; a program needn't handle non-finite values.
Results may differ from the reference program's by a relative error of at most 0.007.
Values may be sent and summed in bfloat16 or wider, within the bound.
A program may use at most 128 MiB of HBM per device.

```python
import math
import jax
import jax.numpy as jnp

D = 12288
HB = 4096
GROUP = 128
TOK = 256
FF = 32768


def touch_ends(drawn, rng, least, largest):
    longest = drawn.shape.index(max(drawn.shape))
    spots = []
    for shift in (0, 1):
        where = [jax.random.randint(jax.random.fold_in(rng, axis), (), 0, length) for axis, length in enumerate(drawn.shape)]
        where[longest] = (where[longest] + shift) % drawn.shape[longest]
        spots.append(tuple(where))
    return drawn.at[spots[0]].set(least).at[spots[1]].set(largest)


def levels(stream_key, shape, cuts, low, largest):
    def one(position, parts):
        heights = jax.random.uniform(jax.random.fold_in(jax.random.fold_in(stream_key, 6), position), (parts,), jnp.float32, low / len(cuts), largest / len(cuts))
        return jnp.repeat(jnp.exp(heights), shape[position] // parts).reshape((-1,) + (1,) * (len(shape) - position - 1))

    gain = one(*cuts[0])
    for cut in cuts[1:]:
        gain = gain * one(*cut)
    return gain


def noise(key, shape, spread, most, shards=(), kind=jnp.bfloat16):
    factor_of = levels(key, shape, shards, -0.22, 0.18) if shards else 1.0
    values = jax.random.normal(key, shape, jnp.float32) * spread * factor_of
    return jnp.minimum(jnp.maximum(values, -most), most).astype(kind)


def setup_inputs(seed: int = 0) -> dict:
    key_of = jax.random.split(jax.random.key(seed), 11)
    return {
        "inputs": noise(key_of[0], (TOK, D), 1.0, 6.0, ((1, 8),)),
        "gate_pre": noise(key_of[1], (TOK, FF), 1.5, 8.0, ((1, 32),)),
        "up_pre": noise(key_of[2], (TOK, FF), 1.0, 6.0, ((1, 32),)),
        "out_grad": noise(key_of[3], (TOK, D), 1.0, 6.0, ((1, 8),)),
        "gate_codes": touch_ends(jax.random.randint(key_of[4], (D // 2, FF), 0, 256), jax.random.fold_in(key_of[4], 1), 0, 255).astype(jnp.int32),
        "up_codes": touch_ends(jax.random.randint(key_of[5], (D // 2, FF), 0, 256), jax.random.fold_in(key_of[5], 1), 0, 255).astype(jnp.int32),
        "down_codes": touch_ends(jax.random.randint(key_of[6], (FF // 2, D), 0, 256), jax.random.fold_in(key_of[6], 1), 0, 255).astype(jnp.int32),
        "gate_scale": jnp.clip(jnp.exp(math.log(0.0027063293) - 0.9162907 * jax.random.uniform(key_of[7], (D // GROUP, FF), jnp.float32) ** levels(key_of[7], (D // GROUP, FF), ((0, 8), (1, 32)), -0.2, 0.2)), 0.0010825318, 0.0027063293),
        "up_scale": jnp.clip(jnp.exp(math.log(0.0027063293) - 0.9162907 * jax.random.uniform(key_of[8], (D // GROUP, FF), jnp.float32) ** levels(key_of[8], (D // GROUP, FF), ((0, 8), (1, 32)), -0.2, 0.2)), 0.0010825318, 0.0027063293),
        "down_scale": jnp.clip(jnp.exp(math.log(0.0016572815) - 0.916290732 * jax.random.uniform(key_of[9], (FF // GROUP, D), jnp.float32) ** levels(key_of[9], (FF // GROUP, D), ((0, 32), (1, 8)), -0.2, 0.2)), 0.0006629126, 0.0016572815),
    }


def unpack_centred(packed):
    shifts = 4 * jnp.arange(2, dtype=jnp.int32)
    nibbles = jnp.bitwise_and(jnp.right_shift(packed[:, None, :], shifts[None, :, None]), 15)
    nibbles = nibbles.reshape(packed.shape[0] * 2, packed.shape[1])
    return (nibbles - 8).astype(jnp.float32)


def dequantize(packed, scales):
    centred = unpack_centred(packed)
    weight = (centred * jnp.repeat(scales, GROUP, axis=0)).astype(jnp.bfloat16)
    return weight, centred


def hadamard(values):
    extent = values.shape[-1]
    result = values
    stride = 1
    while stride < extent:
        result = result.reshape(-1, extent // (2 * stride), 2, stride)
        first = result[:, :, 0]
        second = result[:, :, 1]
        result = jnp.stack([first + second, first - second], axis=2).reshape(-1, extent)
        stride = stride * 2
    return result * (HB ** -0.5)


def group_sum(values, centred, scales):
    rows, cols = values.shape
    return scales * (centred * values).reshape(rows // GROUP, GROUP, cols).sum(axis=1)


def reference(inputs, gate_pre, up_pre, out_grad, gate_codes, up_codes, down_codes, gate_scale, up_scale, down_scale):
    grad_inputs = jnp.zeros((TOK, D), jnp.float32)
    gate_parts = []
    up_parts = []
    down_parts = []
    for block_index in range(FF // HB):
        first_col = block_index * HB
        down_weight, down_centred = dequantize(down_codes[first_col // 2:(first_col + HB) // 2], down_scale[first_col // GROUP:(first_col + HB) // GROUP])
        rotated_grad = jnp.dot(out_grad, down_weight.T, preferred_element_type=jnp.float32).astype(jnp.bfloat16)
        gate_val = gate_pre[:, first_col:first_col + HB].astype(jnp.float32)
        up_val = up_pre[:, first_col:first_col + HB].astype(jnp.float32)
        activated = jax.nn.silu(gate_val)
        hidden = (activated * up_val).astype(jnp.bfloat16)
        rotated = hadamard(hidden.astype(jnp.float32)).astype(jnp.bfloat16)
        hidden_grad = hadamard(rotated_grad.astype(jnp.float32))
        sigmoid_gate = jax.nn.sigmoid(gate_val)
        slope = sigmoid_gate * (1.0 + gate_val * (1.0 - sigmoid_gate))
        gate_grad = (hidden_grad * up_val * slope).astype(jnp.bfloat16)
        up_grad = (hidden_grad * activated).astype(jnp.bfloat16)
        gate_weight, gate_centred = dequantize(gate_codes[:, first_col:first_col + HB], gate_scale[:, first_col:first_col + HB])
        up_weight, up_centred = dequantize(up_codes[:, first_col:first_col + HB], up_scale[:, first_col:first_col + HB])
        grad_inputs = grad_inputs + jnp.dot(gate_grad, gate_weight.T, preferred_element_type=jnp.float32) + jnp.dot(up_grad, up_weight.T, preferred_element_type=jnp.float32)
        gate_full = jnp.dot(inputs.T, gate_grad, preferred_element_type=jnp.float32)
        gate_parts.append(group_sum(gate_full, gate_centred, gate_scale[:, first_col:first_col + HB]))
        up_full = jnp.dot(inputs.T, up_grad, preferred_element_type=jnp.float32)
        up_parts.append(group_sum(up_full, up_centred, up_scale[:, first_col:first_col + HB]))
        down_full = jnp.dot(rotated.T, out_grad, preferred_element_type=jnp.float32)
        down_parts.append(group_sum(down_full, down_centred, down_scale[first_col // GROUP:(first_col + HB) // GROUP]))
    return (grad_inputs.astype(jnp.bfloat16), jnp.concatenate(gate_parts, axis=1), jnp.concatenate(up_parts, axis=1), jnp.concatenate(down_parts, axis=0))
```

```python
import functools
import jax
import jax.numpy as jnp
from jax import lax
from jax.experimental import pallas as pl
from jax.experimental.pallas import tpu as pltpu
from jax.sharding import PartitionSpec as P

HB = 4096
GROUP = 128
SUB = 256
WORDS = SUB // 2
HALF = GROUP // 2
F32 = jnp.float32
BF16 = jnp.bfloat16
NT = (((1,), (1,)), ((), ()))


def parity(v):
    v = jnp.bitwise_xor(v, jnp.right_shift(v, 4))
    v = jnp.bitwise_xor(v, jnp.right_shift(v, 2))
    v = jnp.bitwise_xor(v, jnp.right_shift(v, 1))
    return jnp.bitwise_and(v, 1)


def natural(k):
    return 2 * jnp.bitwise_and(k, WORDS - 1) + jnp.right_shift(k, 7)


def centred_pair(words):
    low = (jnp.bitwise_and(words, 15) - 8).astype(F32)
    high = (jnp.right_shift(words, 4) - 8).astype(F32)
    return low, high


def body(
    dims,
    inp_hbm, gp_hbm, up_hbm, og_hbm, gc_hbm, uc_hbm, dc_hbm, gs_hbm, us_hbm, ds_hbm,
    gi_out, gl_out, ul_out, dl_out,
    inp, gp, up, og, gc, uc, dc, gs, us, ds,
    gw, uw, dw, act, slope, xt, rt, gg, ug,
    hnat, hperm, pick, unpick,
    pbuf, prx, sbuf, xrx, rg, hd, hga, rta, ybuf, yrx, zbuf, zrx,
    load_sem, dc_sem, gc_sem, uc_sem,
    p_s, p_r, x_s, x_r, y_s, y_r, f_s, f_r, ga_s, ga_r, gp_s, gp_r, ra_s, ra_r, rp_s, rp_r,
    ry_s, ry_r, rz_s, rz_r,
):
    NX, NY, NZ, T, D, F = dims
    NB = F // SUB
    NM = D // SUB
    NC = NM // 2
    TS = T // (2 * NX)
    TH = T // 2
    h = lax.axis_index("hid")
    w = lax.axis_index("wid")
    x = w // 2
    core = w % 2
    z = h // NY
    y = h % NY
    mine = core * NX + x

    def x_dev(k):
        return (h, lax.rem(x + k, NX) * 2 + core)

    def y_dev(k):
        return (z * NY + lax.rem(y + k, NY), w)

    def z_dev(k):
        return (lax.rem(z + k, NZ) * NY + y, w)

    partner = (h, x * 2 + 1 - core)

    def remote(src, dst, ssem, rsem, dev):
        return pltpu.make_async_remote_copy(
            src_ref=src, dst_ref=dst, send_sem=ssem, recv_sem=rsem,
            device_id=dev, device_id_type=pl.DeviceIdType.MESH,
        )

    barrier = pltpu.get_barrier_semaphore()
    peers = [partner] + [x_dev(k) for k in range(1, NX)] + [y_dev(k) for k in range(1, NY)]
    peers += [z_dev(k) for k in range(1, NZ)]
    for dev in peers:
        pl.semaphore_signal(barrier, inc=1, device_id=dev, device_id_type=pl.DeviceIdType.MESH)

    my_rows = pl.ds(pl.multiple_of(mine * TS, TS), TS)
    loads = {}

    def load(name, src, dst, idx):
        copy = pltpu.make_async_copy(src, dst, load_sem.at[idx])
        copy.start()
        loads[name] = copy

    def dc_copy(b):
        rows = pl.ds(pl.multiple_of(b * WORDS, WORDS), WORDS)
        return pltpu.make_async_copy(dc_hbm.at[rows], dc.at[rows], dc_sem.at[b])

    def gc_copy(m):
        rows = pl.ds(pl.multiple_of(m * WORDS, WORDS), WORDS)
        return pltpu.make_async_copy(gc_hbm.at[rows], gc.at[rows], gc_sem.at[m])

    def uc_copy(m):
        rows = pl.ds(pl.multiple_of(m * WORDS, WORDS), WORDS)
        return pltpu.make_async_copy(uc_hbm.at[rows], uc.at[rows], uc_sem.at[m])

    load("ds", ds_hbm, ds, 0)
    dc_copy(0).start()
    load("og", og_hbm, og, 1)
    for b in range(1, NB):
        dc_copy(b).start()
    load("gp", gp_hbm, gp, 2)
    load("up", up_hbm, up, 3)
    load("gs", gs_hbm, gs, 4)
    load("us", us_hbm, us, 5)
    for m in range(NM):
        gc_copy(m).start()
        uc_copy(m).start()
    load("inp", inp_hbm, inp, 6)

    row = lax.broadcasted_iota(jnp.int32, (SUB, SUB), 0)
    col = lax.broadcasted_iota(jnp.int32, (SUB, SUB), 1)
    hnat[...] = (1 - 2 * parity(jnp.bitwise_and(row, col))).astype(F32).astype(BF16)
    hperm[...] = (1 - 2 * parity(jnp.bitwise_and(natural(row), col))).astype(F32).astype(BF16)
    pick[...] = (natural(row) == col).astype(F32).astype(BF16)

    def dequant(codes, scales, weights, m, base):
        for g in range(2):
            words = codes[pl.ds(pl.multiple_of(base + g * HALF, HALF), HALF), :]
            low, high = centred_pair(words)
            scale = scales[pl.ds(2 * m + g, 1), :]
            weights[m, g * HALF:(g + 1) * HALF, :] = (low * scale).astype(BF16)
            weights[m, WORDS + g * HALF:WORDS + (g + 1) * HALF, :] = (high * scale).astype(BF16)

    def p_copy(b):
        rows = pl.ds(pl.multiple_of((1 - core) * TH, TH), TH)
        return remote(pbuf.at[b, rows], prx.at[b], p_s.at[b], p_r.at[b], partner)

    def x_copy(b, k):
        rows = pl.ds(pl.multiple_of(lax.rem(x + k, NX) * TS, TS), TS)
        return remote(sbuf.at[b, rows], xrx.at[b, k - 1], x_s.at[b, k - 1], x_r.at[b, k - 1], x_dev(k))

    def y_copy(b, k):
        return remote(rg.at[0, b], rg.at[k, b], y_s.at[b, k - 1], y_r.at[b, k - 1], y_dev(k))

    def f_copy(k):
        return remote(hd.at[0], hd.at[k], f_s.at[k - 1], f_r.at[k - 1], y_dev(k))

    def first_product(b):
        dc_copy(b).wait()
        dequant(dc, ds, dw, b, b * WORDS)
        pbuf[b] = lax.dot_general(og[...], dw[b], NT, preferred_element_type=F32).astype(BF16)

    def pair_sum(b):
        p_copy(b).wait_recv()
        own = pbuf[b, pl.ds(pl.multiple_of(core * TH, TH), TH), :].astype(F32)
        sbuf[b] = (own + prx[b].astype(F32)).astype(BF16)
        for k in range(1, NX):
            x_copy(b, k).start()

    loads["ds"].wait()
    loads["og"].wait()
    first_product(0)
    pl.semaphore_wait(barrier, len(peers))
    p_copy(0).start()

    loads["gp"].wait()
    loads["up"].wait()
    gate = gp[my_rows, :].astype(F32)
    hidden = (gate * (1.0 / (1.0 + jnp.exp(-gate))) * up[my_rows, :].astype(F32)).astype(BF16)
    for b in range(NB):
        hd[0, b] = hidden[:, b * SUB:(b + 1) * SUB]
    for k in range(1, NY):
        f_copy(k).start()

    for b in range(1, NB):
        first_product(b)
        p_copy(b).start()
        pair_sum(b - 1)
    pair_sum(NB - 1)

    @pl.loop(0, T // 32)
    def _(i):
        rows = pl.ds(pl.multiple_of(i * 32, 32), 32)
        g = gp[rows, :].astype(F32)
        sg = 1.0 / (1.0 + jnp.exp(-g))
        act[rows, :] = g * sg
        slope[rows, :] = up[rows, :].astype(F32) * (sg * (1.0 + g * (1.0 - sg)))

    for b in range(NB):
        total = sbuf[b, pl.ds(pl.multiple_of(x * TS, TS), TS), :].astype(F32)
        for k in range(1, NX):
            x_copy(b, k).wait_recv()
            total = total + xrx[b, k - 1].astype(F32)
        rg[0, b] = total.astype(BF16)
        for k in range(1, NY):
            y_copy(b, k).start()

    def sign_of(k):
        source = lax.rem(y + NY - k, NY)
        both = jnp.bitwise_and(source, y)
        odd = jnp.bitwise_and(jnp.bitwise_xor(both, jnp.right_shift(both, 1)), 1)
        return (1 - 2 * odd).astype(F32)

    def rotate(parts, signs):
        turned = jnp.dot(
            parts[...].reshape(NY * NB * TS, SUB), signs[...], preferred_element_type=F32
        ).reshape(NY, NB, TS, SUB)
        total = turned[0] * sign_of(0)
        for k in range(1, NY):
            total = total + turned[k] * sign_of(k)
        pieces = [total[b] for b in range(NB)]
        step = 1
        while step < NB:
            fresh = list(pieces)
            for b in range(NB):
                if b & step:
                    fresh[b] = pieces[b - step] - pieces[b]
                else:
                    fresh[b] = pieces[b] + pieces[b + step]
            pieces = fresh
            step = step * 2
        return jnp.concatenate(pieces, axis=1) * (HB ** -0.5)

    def spread_x(buf, ssem, rsem, k):
        return remote(buf.at[mine], buf.at[mine], ssem.at[k - 1], rsem.at[k - 1], x_dev(k))

    def slot_from(k):
        return core * NX + lax.rem(x + NX - k, NX)

    def slot_of_partner(k):
        return (1 - core) * NX + lax.rem(x + NX - k, NX)

    def spread_pair(buf, ssem, rsem, k):
        slot = slot_from(k)
        return remote(buf.at[slot], buf.at[slot], ssem.at[k], rsem.at[k], partner)

    def spread(buf, xs, xr, ps, pr):
        for k in range(1, NX):
            spread_x(buf, xs, xr, k).start()
        spread_pair(buf, ps, pr, 0).start()

    for k in range(1, NY):
        f_copy(k).wait_recv()
    rta[mine] = rotate(hd, hnat).astype(BF16)
    spread(rta, ra_s, ra_r, rp_s, rp_r)

    loads["gs"].wait()
    loads["us"].wait()

    @pl.loop(0, NM)
    def _(m):
        gc_copy(m).wait()
        dequant(gc, gs, gw, m, m * WORDS)

    for b in range(NB):
        for k in range(1, NY):
            y_copy(b, k).wait_recv()
    hga[mine] = rotate(rg, hperm).astype(BF16)
    spread(hga, ga_s, ga_r, gp_s, gp_r)

    for k in range(1, NX):
        spread_x(rta, ra_s, ra_r, k).wait_recv()
        spread_pair(rta, rp_s, rp_r, k).start()

    @pl.loop(0, NM)
    def _(m):
        uc_copy(m).wait()
        dequant(uc, us, uw, m, m * WORDS)

    def grads(slot):
        rows = pl.ds(pl.multiple_of(slot * TS, TS), TS)
        hg = hga[slot].astype(F32)
        gg[rows, :] = (hg * slope[rows, :]).astype(BF16)
        ug[rows, :] = (hg * act[rows, :]).astype(BF16)

    grads(mine)
    for k in range(1, NX):
        spread_x(hga, ga_s, ga_r, k).wait_recv()
        spread_pair(hga, gp_s, gp_r, k).start()
        grads(slot_from(k))
    for k in range(NX):
        slot = slot_of_partner(k)
        remote(hga.at[slot], hga.at[slot], gp_s.at[k], gp_r.at[k], partner).wait_recv()
        grads(slot)

    def ry_copy(n, k):
        return remote(ybuf.at[n, lax.rem(y + k, NY)], yrx.at[n, k - 1], ry_s.at[n, k - 1], ry_r.at[n, k - 1], y_dev(k))

    def rz_copy(n, k):
        return remote(zbuf.at[n, lax.rem(z + k, NZ)], zrx.at[n, k - 1], rz_s.at[n, k - 1], rz_r.at[n, k - 1], z_dev(k))

    @pl.loop(0, NC)
    def _(n):
        for sub in range(2):
            m = 2 * n + sub
            both = lax.dot_general(gg[...], gw[m], NT, preferred_element_type=F32)
            both = both + lax.dot_general(ug[...], uw[m], NT, preferred_element_type=F32)
            both = both.reshape(NZ, NY, 8, SUB)
            for t in range(NY):
                ybuf[n, t, :, sub * SUB:(sub + 1) * SUB] = both[:, t].reshape(NZ * 8, SUB).astype(BF16)
        for k in range(1, NY):
            ry_copy(n, k).start()

    def y_sum(n):
        total = ybuf[n, y].astype(F32)
        for k in range(1, NY):
            ry_copy(n, k).wait_recv()
            total = total + yrx[n, k - 1].astype(F32)
        zbuf[n] = total.reshape(NZ, 8, 2 * SUB).astype(BF16)
        for k in range(1, NZ):
            rz_copy(n, k).start()

    def flip(block):
        return lax.dot_general(pick[...], block, NT, preferred_element_type=F32).astype(BF16)

    def group_sums(codes, left, right, scales, out, j, count):
        cols = pl.ds(pl.multiple_of(j * SUB, SUB), SUB)
        for m in range(count):
            full = jnp.dot(left[m], right[:, cols], preferred_element_type=F32)
            low, high = centred_pair(codes[m * WORDS:(m + 1) * WORDS, cols])
            prod = full[:WORDS] * low + full[WORDS:] * high
            for g in range(2):
                line = jnp.sum(prod[g * HALF:(g + 1) * HALF], axis=0, keepdims=True)
                out[2 * m + g:2 * m + g + 1, cols] = line * scales[2 * m + g:2 * m + g + 1, cols]

    loads["inp"].wait()
    for m in range(NM):
        xt[m] = flip(inp[:, m * SUB:(m + 1) * SUB])

    @pl.loop(0, F // SUB)
    def _(j):
        group_sums(gc, xt, gg, gs, gl_out, j, NM)

    for n in range(NC):
        y_sum(n)

    @pl.loop(0, F // SUB)
    def _(j):
        group_sums(uc, xt, ug, us, ul_out, j, NM)

    for k in range(NX):
        slot = slot_of_partner(k)
        remote(rta.at[slot], rta.at[slot], rp_s.at[k], rp_r.at[k], partner).wait_recv()
    whole = rta[...].reshape(T, F)
    for b in range(NB):
        rt[b] = flip(whole[:, b * SUB:(b + 1) * SUB])

    @pl.loop(0, D // SUB)
    def _(j):
        group_sums(dc, rt, og, ds, dl_out, j, NB)

    for n in range(NC):
        total = zbuf[n, z].astype(F32)
        for k in range(1, NZ):
            rz_copy(n, k).wait_recv()
            total = total + zrx[n, k - 1].astype(F32)
        for sub in range(2):
            unpick[2 * n + sub] = total[:, sub * SUB:(sub + 1) * SUB]
    ordered = jnp.dot(
        unpick[...].reshape(NM * 8, SUB).astype(BF16), pick[...], preferred_element_type=F32
    ).astype(BF16).astype(F32).reshape(NM, 8, SUB)
    for m in range(NM):
        gi_out[:, m * SUB:(m + 1) * SUB] = ordered[m].astype(BF16)

    for b in range(NB):
        p_copy(b).wait_send()
        for k in range(1, NX):
            x_copy(b, k).wait_send()
        for k in range(1, NY):
            y_copy(b, k).wait_send()
    for k in range(1, NY):
        f_copy(k).wait_send()
    for k in range(1, NX):
        spread_x(rta, ra_s, ra_r, k).wait_send()
        spread_x(hga, ga_s, ga_r, k).wait_send()
    for k in range(NX):
        spread_pair(rta, rp_s, rp_r, k).wait_send()
        spread_pair(hga, gp_s, gp_r, k).wait_send()
    for n in range(NC):
        for k in range(1, NY):
            ry_copy(n, k).wait_send()
        for k in range(1, NZ):
            rz_copy(n, k).wait_send()


def shards(hid, wid, inputs, gate_pre, up_pre, out_grad, gate_codes, up_codes, down_codes, gate_scale, up_scale, down_scale):
    T, D = inputs.shape
    F = gate_pre.shape[1]
    NY = HB // F
    NZ = hid // NY
    NX = wid // 2
    NB, NM = F // SUB, D // SUB
    NC = NM // 2
    TS, TH = T // wid, T // 2
    V = pltpu.VMEM
    dma = lambda *shape: pltpu.SemaphoreType.DMA(shape)
    scratch = [
        V((T, D), BF16), V((T, F), BF16), V((T, F), BF16), V((T, D), BF16),
        V((D // 2, F), jnp.int32), V((D // 2, F), jnp.int32), V((F // 2, D), jnp.int32),
        V(gate_scale.shape, F32), V(up_scale.shape, F32), V(down_scale.shape, F32),
        V((NM, SUB, F), BF16), V((NM, SUB, F), BF16), V((NB, SUB, D), BF16),
        V((T, F), F32), V((T, F), F32),
        V((NM, SUB, T), BF16), V((NB, SUB, T), BF16),
        V((T, F), BF16), V((T, F), BF16),
        V((SUB, SUB), BF16), V((SUB, SUB), BF16), V((SUB, SUB), BF16), V((NM, 8, SUB), F32),
        V((NB, T, SUB), BF16), V((NB, TH, SUB), BF16), V((NB, TH, SUB), BF16),
        V((NB, NX - 1, TS, SUB), BF16),
        V((NY, NB, TS, SUB), BF16), V((NY, NB, TS, SUB), BF16),
        V((wid, TS, F), BF16), V((wid, TS, F), BF16),
        V((NC, NY, NZ * 8, 2 * SUB), BF16), V((NC, NY - 1, NZ * 8, 2 * SUB), BF16),
        V((NC, NZ, 8, 2 * SUB), BF16), V((NC, NZ - 1, 8, 2 * SUB), BF16),
        dma(7), dma(NB), dma(NM), dma(NM),
        dma(NB), dma(NB), dma(NB, NX - 1), dma(NB, NX - 1), dma(NB, NY - 1), dma(NB, NY - 1),
        dma(NY - 1), dma(NY - 1),
        dma(NX - 1), dma(NX - 1), dma(NX), dma(NX), dma(NX - 1), dma(NX - 1), dma(NX), dma(NX),
        dma(NC, NY - 1), dma(NC, NY - 1), dma(NC, NZ - 1), dma(NC, NZ - 1),
    ]
    return pl.pallas_call(
        functools.partial(body, (NX, NY, NZ, T, D, F)),
        out_shape=(
            jax.ShapeDtypeStruct((T // hid, D), BF16),
            jax.ShapeDtypeStruct(gate_scale.shape, F32),
            jax.ShapeDtypeStruct(up_scale.shape, F32),
            jax.ShapeDtypeStruct(down_scale.shape, F32),
        ),
        in_specs=[pl.BlockSpec(memory_space=pl.ANY)] * 10,
        out_specs=[pl.BlockSpec(memory_space=pltpu.VMEM)] * 4,
        scratch_shapes=scratch,
        compiler_params=pltpu.CompilerParams(
            collective_id=0, has_side_effects=True, vmem_limit_bytes=60 * 1024 * 1024
        ),
        name="layer",
    )(inputs, gate_pre, up_pre, out_grad, gate_codes, up_codes, down_codes, gate_scale, up_scale, down_scale)


def solution(mesh):
    in_specs = (
        P(None, "wid"),
        P(None, "hid"),
        P(None, "hid"),
        P(None, "wid"),
        P("wid", "hid"),
        P("wid", "hid"),
        P("hid", "wid"),
        P("wid", "hid"),
        P("wid", "hid"),
        P("hid", "wid"),
    )
    out_specs = (P("hid", "wid"), P("wid", "hid"), P("wid", "hid"), P("hid", "wid"))
    fn = functools.partial(shards, mesh.shape["hid"], mesh.shape["wid"])
    return jax.shard_map(fn, mesh=mesh, in_specs=in_specs, out_specs=out_specs, check_vma=False)
```

```python
import functools
import jax
import jax.numpy as jnp
from jax import lax
from jax.experimental import pallas as pl
from jax.experimental.pallas import tpu as pltpu
from jax.sharding import PartitionSpec as P

HB = 4096
GROUP = 128
SUB = 256
WORDS = SUB // 2
HALF = GROUP // 2
F32 = jnp.float32
BF16 = jnp.bfloat16
NT = (((1,), (1,)), ((), ()))


def parity(v):
    v = jnp.bitwise_xor(v, jnp.right_shift(v, 4))
    v = jnp.bitwise_xor(v, jnp.right_shift(v, 2))
    v = jnp.bitwise_xor(v, jnp.right_shift(v, 1))
    return jnp.bitwise_and(v, 1)


def natural(k):
    return 2 * jnp.bitwise_and(k, WORDS - 1) + jnp.right_shift(k, 7)


def centred_pair(words):
    low = (jnp.bitwise_and(words, 15) - 8).astype(F32)
    high = (jnp.right_shift(words, 4) - 8).astype(F32)
    return low, high


def body(
    dims,
    inp_hbm, gp_hbm, up_hbm, og_hbm, gc_hbm, uc_hbm, dc_hbm, gs_hbm, us_hbm, ds_hbm,
    gi_out, gl_out, ul_out, dl_out,
    inp, gp, up, og, gc, uc, dc, gs, us, ds,
    gw, uw, dw, gwt, uwt, act, slope, xt, rt, gg, ug,
    hnat, hperm, pick, eye, unpick,
    pbuf, prx, sbuf, xrx, rg, hd, hga, rta, ybuf, yrx, zbuf, zrx,
    load_sem, dc_sem,
    p_s, p_r, x_s, x_r, y_s, y_r, f_s, f_r, ga_s, ga_r, gp_s, gp_r, ra_s, ra_r, rp_s, rp_r,
    ry_s, ry_r, rz_s, rz_r,
):
    NX, NY, NZ, T, D, F = dims
    NB = F // SUB
    NM = D // SUB
    TS = T // (2 * NX)
    TH = T // 2
    h = lax.axis_index("hid")
    w = lax.axis_index("wid")
    x = w // 2
    core = w % 2
    z = h // NY
    y = h % NY
    mine = core * NX + x

    def x_dev(k):
        return (h, lax.rem(x + k, NX) * 2 + core)

    def y_dev(k):
        return (z * NY + lax.rem(y + k, NY), w)

    def z_dev(k):
        return (lax.rem(z + k, NZ) * NY + y, w)

    partner = (h, x * 2 + 1 - core)
    near = [1, NX - 1] if NX > 2 else []
    far = NX // 2

    def remote(src, dst, ssem, rsem, dev):
        return pltpu.make_async_remote_copy(
            src_ref=src, dst_ref=dst, send_sem=ssem, recv_sem=rsem,
            device_id=dev, device_id_type=pl.DeviceIdType.MESH,
        )

    def all_of(ref, sem):
        pltpu.make_async_copy(ref, ref, sem).wait()

    barrier = pltpu.get_barrier_semaphore()
    peers = [partner] + [x_dev(k) for k in range(1, NX)] + [y_dev(k) for k in range(1, NY)]
    peers += [z_dev(k) for k in range(1, NZ)]
    for dev in peers:
        pl.semaphore_signal(barrier, inc=1, device_id=dev, device_id_type=pl.DeviceIdType.MESH)

    my_rows = pl.ds(pl.multiple_of(mine * TS, TS), TS)
    loads = {}

    def load(name, src, dst, idx):
        copy = pltpu.make_async_copy(src, dst, load_sem.at[idx])
        copy.start()
        loads[name] = copy

    def dc_copy(b):
        rows = pl.ds(pl.multiple_of(b * WORDS, WORDS), WORDS)
        return pltpu.make_async_copy(dc_hbm.at[rows], dc.at[rows], dc_sem.at[b])

    load("ds", ds_hbm, ds, 0)
    dc_copy(0).start()
    load("og", og_hbm, og, 1)
    for b in range(1, NB):
        dc_copy(b).start()
    load("gp", gp_hbm, gp, 2)
    load("up", up_hbm, up, 3)

    row = lax.broadcasted_iota(jnp.int32, (SUB, SUB), 0)
    col = lax.broadcasted_iota(jnp.int32, (SUB, SUB), 1)
    hnat[...] = (1 - 2 * parity(jnp.bitwise_and(row, col))).astype(F32).astype(BF16)
    hperm[...] = (1 - 2 * parity(jnp.bitwise_and(natural(row), col))).astype(F32).astype(BF16)
    eye[...] = (row == col).astype(F32).astype(BF16)
    pick[...] = (natural(row) == col).astype(F32).astype(BF16)

    def dequant(codes, scales, weights, m, base):
        for g in range(2):
            words = codes[base + g * HALF:base + (g + 1) * HALF, :]
            low, high = centred_pair(words)
            scale = scales[2 * m + g:2 * m + g + 1, :]
            weights[m, g * HALF:(g + 1) * HALF, :] = (low * scale).astype(BF16)
            weights[m, WORDS + g * HALF:WORDS + (g + 1) * HALF, :] = (high * scale).astype(BF16)

    def p_copy(b):
        rows = pl.ds(pl.multiple_of((1 - core) * TH, TH), TH)
        return remote(pbuf.at[b, rows], prx.at[b], p_s, p_r.at[b], partner)

    def x_copy(b, k):
        rows = pl.ds(pl.multiple_of(lax.rem(x + k, NX) * TS, TS), TS)
        return remote(sbuf.at[b, rows], xrx.at[b, k - 1], x_s, x_r.at[b], x_dev(k))

    def y_copy(b, k):
        return remote(rg.at[0, b], rg.at[k, b], y_s, y_r, y_dev(k))

    def f_copy(k):
        return remote(hd.at[0], hd.at[k], f_s, f_r, y_dev(k))

    def first_product(b):
        if b:
            dc_copy(b).wait()
        dequant(dc, ds, dw, b, b * WORDS)
        pbuf[b] = lax.dot_general(og[...], dw[b], NT, preferred_element_type=F32).astype(BF16)

    def pair_sum(b):
        p_copy(b).wait_recv()
        own = pbuf[b, pl.ds(pl.multiple_of(core * TH, TH), TH), :].astype(F32)
        sbuf[b] = (own + prx[b].astype(F32)).astype(BF16)
        for k in range(1, NX):
            x_copy(b, k).start()

    loads["ds"].wait()
    loads["og"].wait()
    dc_copy(0).wait()
    first_product(0)
    load("gs", gs_hbm, gs, 4)
    load("us", us_hbm, us, 5)
    load("gc", gc_hbm, gc, 7)
    load("uc", uc_hbm, uc, 8)
    load("inp", inp_hbm, inp, 6)
    pl.semaphore_wait(barrier, len(peers))
    p_copy(0).start()

    loads["gp"].wait()
    loads["up"].wait()
    gate = gp[my_rows, :].astype(F32)
    hidden = (gate * (1.0 / (1.0 + jnp.exp(-gate))) * up[my_rows, :].astype(F32)).astype(BF16)
    for b in range(NB):
        hd[0, b] = hidden[:, b * SUB:(b + 1) * SUB]
    for k in range(1, NY):
        f_copy(k).start()

    for b in range(1, NB):
        first_product(b)
        p_copy(b).start()
        if b >= 2:
            pair_sum(b - 2)
    pair_sum(NB - 2)
    pair_sum(NB - 1)

    @pl.loop(0, T // 32)
    def _(i):
        rows = pl.ds(pl.multiple_of(i * 32, 32), 32)
        g = gp[rows, :].astype(F32)
        sg = 1.0 / (1.0 + jnp.exp(-g))
        act[rows, :] = g * sg
        slope[rows, :] = up[rows, :].astype(F32) * (sg * (1.0 + g * (1.0 - sg)))

    def sign_of(k):
        source = lax.rem(y + NY - k, NY)
        both = jnp.bitwise_and(source, y)
        odd = jnp.bitwise_and(jnp.bitwise_xor(both, jnp.right_shift(both, 1)), 1)
        return (1 - 2 * odd).astype(F32)

    def rotate(parts, signs):
        turned = jnp.dot(
            parts[...].reshape(NY * NB * TS, SUB), signs[...], preferred_element_type=F32
        ).reshape(NY, NB, TS, SUB)
        total = turned[0] * sign_of(0)
        for k in range(1, NY):
            total = total + turned[k] * sign_of(k)
        pieces = [total[b] for b in range(NB)]
        step = 1
        while step < NB:
            fresh = list(pieces)
            for b in range(NB):
                if b & step:
                    fresh[b] = pieces[b - step] - pieces[b]
                else:
                    fresh[b] = pieces[b] + pieces[b + step]
            pieces = fresh
            step = step * 2
        return jnp.concatenate(pieces, axis=1) * (HB ** -0.5)

    def spread_x(buf, ssem, rsem, k):
        return remote(buf.at[mine], buf.at[mine], ssem, rsem, x_dev(k))

    def slot_from(k):
        return core * NX + lax.rem(x + NX - k, NX)

    def slot_of_partner(k):
        return (1 - core) * NX + lax.rem(x + NX - k, NX)

    def spread_pair(buf, ssem, rsem, k):
        slot = slot_from(k)
        return remote(buf.at[slot], buf.at[slot], ssem, rsem, partner)

    def spread(buf, xs, xr, ps, pr):
        for k in near + [far]:
            spread_x(buf, xs, xr(k), k).start()
        spread_pair(buf, ps, pr(0), 0).start()

    loads["gs"].wait()
    loads["us"].wait()
    loads["gc"].wait()

    def turn(weights, turned, m):
        for f in range(F // SUB):
            block = weights[m, :, f * SUB:(f + 1) * SUB]
            across = lax.dot_general(eye[...], block, NT, preferred_element_type=F32)
            turned[f * SUB:(f + 1) * SUB, m * SUB:(m + 1) * SUB] = across.astype(BF16)

    def prepare(codes, scales, weights, turned):
        for m in range(NM):
            dequant(codes, scales, weights, m, m * WORDS)
            if m:
                turn(weights, turned, m - 1)
        turn(weights, turned, NM - 1)

    prepare(gc, gs, gw, gwt)

    all_of(hd.at[pl.ds(1, NY - 1)], f_r)
    rta[mine] = rotate(hd, hnat).astype(BF16)
    spread(rta, ra_s, lambda k: ra_r, rp_s, lambda k: rp_r)

    for b in range(NB):
        total = sbuf[b, pl.ds(pl.multiple_of(x * TS, TS), TS), :].astype(F32)
        all_of(xrx.at[b], x_r.at[b])
        for k in range(1, NX):
            total = total + xrx[b, k - 1].astype(F32)
        rg[0, b] = total.astype(BF16)
        for k in range(1, NY):
            y_copy(b, k).start()

    def flip(block):
        return lax.dot_general(pick[...], block, NT, preferred_element_type=F32).astype(BF16)

    def group_sums(codes, left, right, scales, out, j, count):
        cols = pl.ds(pl.multiple_of(j * SUB, SUB), SUB)
        for m in range(count):
            full = jnp.dot(left[m], right[:, cols], preferred_element_type=F32)
            low, high = centred_pair(codes[m * WORDS:(m + 1) * WORDS, cols])
            prod = full[:WORDS] * low + full[WORDS:] * high
            for g in range(2):
                line = jnp.sum(prod[g * HALF:(g + 1) * HALF], axis=0, keepdims=True)
                out[2 * m + g:2 * m + g + 1, cols] = line * scales[2 * m + g:2 * m + g + 1, cols]

    loads["uc"].wait()
    prepare(uc, us, uw, uwt)

    all_of(rg.at[pl.ds(1, NY - 1)], y_r)
    hga[mine] = rotate(rg, hperm).astype(BF16)
    spread(hga, ga_s, lambda k: ga_r.at[k - 1], gp_s, lambda k: gp_r.at[k])

    def ry_copy(slot, half, k):
        cols = pl.ds(half * D // 2, D // 2)
        return remote(
            ybuf.at[slot, lax.rem(y + k, NY), :, cols], yrx.at[slot, k - 1, :, cols],
            ry_s, ry_r.at[slot], y_dev(k),
        )

    def rz_copy(k):
        return remote(zbuf.at[lax.rem(z + k, NZ)], zrx.at[k - 1], rz_s, rz_r, z_dev(k))

    def slot_rows(slot):
        return pl.ds(pl.multiple_of(slot * TS, TS), TS)

    def factors(slots):
        for slot in slots:
            rows = slot_rows(slot)
            hg = hga[slot].astype(F32)
            gg[rows, :] = (hg * slope[rows, :]).astype(BF16)
            ug[rows, :] = (hg * act[rows, :]).astype(BF16)

    def products(slots, half):
        for m in range(half * NM // 2, (half + 1) * NM // 2):
            left = jnp.concatenate([gg[slot_rows(slot), :] for slot in slots], axis=0)
            both = jnp.dot(left, gwt[:, m * SUB:(m + 1) * SUB], preferred_element_type=F32)
            left = jnp.concatenate([ug[slot_rows(slot), :] for slot in slots], axis=0)
            both = both + jnp.dot(left, uwt[:, m * SUB:(m + 1) * SUB], preferred_element_type=F32)
            for i, slot in enumerate(slots):
                piece = both[i * TS:(i + 1) * TS].reshape(NY, 8, SUB).astype(BF16)
                ybuf[slot, :, :, m * SUB:(m + 1) * SUB] = piece
        for slot in slots:
            for k in range(1, NY):
                ry_copy(slot, half, k).start()

    def y_sum(slot):
        total = ybuf[slot, y].astype(F32)
        all_of(yrx.at[slot], ry_r.at[slot])
        for k in range(1, NY):
            total = total + yrx[slot, k - 1].astype(F32)
        zbuf[slot] = total.astype(BF16)

        @pl.when(slot != z)
        def _():
            rz_copy(lax.rem(slot - z + NZ, NZ)).start()

    def from_x(k):
        spread_x(hga, ga_s, ga_r.at[k - 1], k).wait_recv()
        spread_pair(hga, gp_s, gp_r.at[k], k).start()

    def from_pair(k):
        slot = slot_of_partner(k)
        remote(hga.at[slot], hga.at[slot], gp_s, gp_r.at[k], partner).wait_recv()


    all_of(rta.at[pl.ds(0, NX - 1)], ra_r)
    for k in range(1, NX):
        spread_pair(rta, rp_s, rp_r, k).start()
    loads["inp"].wait()
    for m in range(NM):
        xt[m] = flip(inp[:, m * SUB:(m + 1) * SUB])
    first = [mine, slot_of_partner(0)]
    second = [slot_from(k) for k in near]
    third = [slot_of_partner(k) for k in near] + [slot_from(far), slot_of_partner(far)]
    groups = [first, second, third] if near else [first, third]
    from_pair(0)
    factors(first)
    products(first, 0)
    products(first, 1)
    for k in near:
        from_x(k)
    if near:
        factors(second)
        products(second, 0)
    from_x(far)
    if near:
        products(second, 1)
    for k in near:
        from_pair(k)
    from_pair(far)
    factors(third)
    products(third, 0)
    products(third, 1)

    def y_sums(i):
        if i < len(groups):
            for slot in groups[i]:
                y_sum(slot)

    y_sums(0)
    all_of(rta.at[pl.ds(0, NX)], rp_r)
    whole = rta[...].reshape(T, F)
    for b in range(NB):
        rt[b] = flip(whole[:, b * SUB:(b + 1) * SUB])

    @pl.loop(0, D // SUB)
    def _(j):
        group_sums(dc, rt, og, ds, dl_out, j, NB)

    y_sums(1)
    @pl.loop(0, F // SUB)
    def _(j):
        group_sums(gc, xt, gg, gs, gl_out, j, NM)

    y_sums(2)
    @pl.loop(0, F // SUB)
    def _(j):
        group_sums(uc, xt, ug, us, ul_out, j, NM)

    total = zbuf[z].astype(F32)
    all_of(zrx, rz_r)
    for k in range(1, NZ):
        total = total + zrx[k - 1].astype(F32)
    for m in range(NM):
        unpick[m] = total[:, m * SUB:(m + 1) * SUB]
    ordered = jnp.dot(
        unpick[...].reshape(NM * 8, SUB).astype(BF16), pick[...], preferred_element_type=F32
    ).astype(BF16).astype(F32).reshape(NM, 8, SUB)
    for m in range(NM):
        gi_out[:, m * SUB:(m + 1) * SUB] = ordered[m].astype(BF16)

    all_of(prx, p_s)
    all_of(xrx, x_s)
    all_of(rg.at[pl.ds(1, NY - 1)], y_s)
    all_of(hd.at[pl.ds(1, NY - 1)], f_s)
    all_of(rta.at[pl.ds(0, NX - 1)], ra_s)
    all_of(hga.at[pl.ds(0, NX - 1)], ga_s)
    all_of(rta.at[pl.ds(0, NX)], rp_s)
    all_of(hga.at[pl.ds(0, NX)], gp_s)
    all_of(yrx, ry_s)
    all_of(zrx, rz_s)


def hand_out(*refs):
    sem = refs[8]
    copies = [pltpu.make_async_copy(refs[i], refs[4 + i], sem.at[i]) for i in range(4)]
    for copy in copies:
        copy.start()
    for copy in copies:
        copy.wait()


def shards(hid, wid, inputs, gate_pre, up_pre, out_grad, gate_codes, up_codes, down_codes, gate_scale, up_scale, down_scale):
    T, D = inputs.shape
    F = gate_pre.shape[1]
    NY = HB // F
    NZ = hid // NY
    NX = wid // 2
    NB, NM = F // SUB, D // SUB
    TS, TH = T // wid, T // 2
    V = pltpu.VMEM
    dma = lambda *shape: pltpu.SemaphoreType.DMA(shape)
    one = pltpu.SemaphoreType.DMA
    scratch = [
        V((T, D), BF16), V((T, F), BF16), V((T, F), BF16), V((T, D), BF16),
        V((D // 2, F), jnp.int32), V((D // 2, F), jnp.int32), V((F // 2, D), jnp.int32),
        V(gate_scale.shape, F32), V(up_scale.shape, F32), V(down_scale.shape, F32),
        V((NM, SUB, F), BF16), V((NM, SUB, F), BF16), V((NB, SUB, D), BF16), V((F, D), BF16), V((F, D), BF16),
        V((T, F), F32), V((T, F), F32),
        V((NM, SUB, T), BF16), V((NB, SUB, T), BF16),
        V((T, F), BF16), V((T, F), BF16),
        V((SUB, SUB), BF16), V((SUB, SUB), BF16), V((SUB, SUB), BF16), V((SUB, SUB), BF16), V((NM, 8, SUB), F32),
        V((NB, T, SUB), BF16), V((NB, TH, SUB), BF16), V((NB, TH, SUB), BF16),
        V((NB, NX - 1, TS, SUB), BF16),
        V((NY, NB, TS, SUB), BF16), V((NY, NB, TS, SUB), BF16),
        V((wid, TS, F), BF16), V((wid, TS, F), BF16),
        V((wid, NY, 8, D), BF16), V((wid, NY - 1, 8, D), BF16),
        V((NZ, 8, D), BF16), V((NZ - 1, 8, D), BF16),
        dma(9), dma(NB),
        one, dma(NB), one, dma(NB), one, one, one, one,
        one, dma(NX - 1), one, dma(NX), one, one, one, one,
        one, dma(wid), one, one,
    ]
    results = pl.pallas_call(
        functools.partial(body, (NX, NY, NZ, T, D, F)),
        out_shape=(
            V((T // hid, D), BF16), V(gate_scale.shape, F32), V(up_scale.shape, F32), V(down_scale.shape, F32),
        ),
        in_specs=[pl.BlockSpec(memory_space=pl.ANY)] * 10,
        out_specs=[pl.BlockSpec(memory_space=pltpu.VMEM)] * 4,
        scratch_shapes=scratch,
        compiler_params=pltpu.CompilerParams(
            collective_id=0, has_side_effects=True, vmem_limit_bytes=60 * 1024 * 1024
        ),
        name="layer",
    )(inputs, gate_pre, up_pre, out_grad, gate_codes, up_codes, down_codes, gate_scale, up_scale, down_scale)
    return pl.pallas_call(
        hand_out,
        out_shape=[jax.ShapeDtypeStruct(r.shape, r.dtype) for r in results],
        in_specs=[pl.BlockSpec(memory_space=pltpu.VMEM)] * 4,
        out_specs=[pl.BlockSpec(memory_space=pl.ANY)] * 4,
        scratch_shapes=[dma(4)],
        name="hand_out",
    )(*[pltpu.with_memory_space_constraint(r, pltpu.VMEM) for r in results])


def solution(mesh):
    in_specs = (
        P(None, "wid"),
        P(None, "hid"),
        P(None, "hid"),
        P(None, "wid"),
        P("wid", "hid"),
        P("wid", "hid"),
        P("hid", "wid"),
        P("wid", "hid"),
        P("wid", "hid"),
        P("hid", "wid"),
    )
    out_specs = (P("hid", "wid"), P("wid", "hid"), P("wid", "hid"), P("hid", "wid"))
    fn = functools.partial(shards, mesh.shape["hid"], mesh.shape["wid"])
    return jax.shard_map(fn, mesh=mesh, in_specs=in_specs, out_specs=out_specs, check_vma=False)
```

```python
import functools
import jax
import jax.numpy as jnp
from jax import lax
from jax.experimental import pallas as pl
from jax.experimental.pallas import tpu as pltpu
from jax.sharding import PartitionSpec as P

HB = 4096
GROUP = 128
SUB = 256
WORDS = SUB // 2
HALF = GROUP // 2
F32 = jnp.float32
BF16 = jnp.bfloat16
NT = (((1,), (1,)), ((), ()))


def parity(v):
    v = jnp.bitwise_xor(v, jnp.right_shift(v, 4))
    v = jnp.bitwise_xor(v, jnp.right_shift(v, 2))
    v = jnp.bitwise_xor(v, jnp.right_shift(v, 1))
    return jnp.bitwise_and(v, 1)


def natural(k):
    return 2 * jnp.bitwise_and(k, WORDS - 1) + jnp.right_shift(k, 7)


def centred_pair(words):
    low = (jnp.bitwise_and(words, 15) - 8).astype(F32)
    high = (jnp.right_shift(words, 4) - 8).astype(F32)
    return low, high


def body(
    dims,
    inp_hbm, gp_hbm, up_hbm, og_hbm, gc_hbm, uc_hbm, dc_hbm, gs_hbm, us_hbm, ds_hbm,
    gi_out, gl_out, ul_out, dl_out,
    inp, gp, up, og, gc, uc, dc, gs, us, ds,
    gw, uw, dw, gwt, uwt, act, slope, xt, rt, gg, ug,
    hnat, hperm, pick, eye, unpick,
    pbuf, prx, sbuf, xrx, rg, hd, hga, rta, ybuf, yrx, zbuf, zrx,
    load_sem, dc_sem,
    p_s, p_r, x_s, x_r, y_s, y_r, f_s, f_r, ga_s, ga_r, gp_s, gp_r, ra_s, ra_r, rp_s, rp_r,
    ry_s, ry_r, rz_s, rz_r,
):
    NX, NY, NZ, T, D, F = dims
    NB = F // SUB
    NM = D // SUB
    TS = T // (2 * NX)
    TH = T // 2
    h = lax.axis_index("hid")
    w = lax.axis_index("wid")
    x = w // 2
    core = w % 2
    z = h // NY
    y = h % NY
    mine = core * NX + x

    def x_dev(k):
        return (h, lax.rem(x + k, NX) * 2 + core)

    def y_dev(k):
        return (z * NY + lax.rem(y + k, NY), w)

    def z_dev(k):
        return (lax.rem(z + k, NZ) * NY + y, w)

    partner = (h, x * 2 + 1 - core)
    near = [1, NX - 1] if NX > 2 else []
    far = NX // 2

    def remote(src, dst, ssem, rsem, dev):
        return pltpu.make_async_remote_copy(
            src_ref=src, dst_ref=dst, send_sem=ssem, recv_sem=rsem,
            device_id=dev, device_id_type=pl.DeviceIdType.MESH,
        )

    def all_of(ref, sem):
        pltpu.make_async_copy(ref, ref, sem).wait()

    barrier = pltpu.get_barrier_semaphore()
    peers = [partner] + [x_dev(k) for k in range(1, NX)] + [y_dev(k) for k in range(1, NY)]
    peers += [z_dev(k) for k in range(1, NZ)]
    for dev in peers:
        pl.semaphore_signal(barrier, inc=1, device_id=dev, device_id_type=pl.DeviceIdType.MESH)

    my_rows = pl.ds(pl.multiple_of(mine * TS, TS), TS)
    loads = {}

    def load(name, src, dst, idx):
        copy = pltpu.make_async_copy(src, dst, load_sem.at[idx])
        copy.start()
        loads[name] = copy

    def dc_copy(b):
        rows = pl.ds(pl.multiple_of(b * WORDS, WORDS), WORDS)
        return pltpu.make_async_copy(dc_hbm.at[rows], dc.at[rows], dc_sem.at[b])

    load("ds", ds_hbm, ds, 0)
    dc_copy(0).start()
    load("og", og_hbm, og, 1)
    for b in range(1, NB):
        dc_copy(b).start()
    load("gp", gp_hbm, gp, 2)
    load("up", up_hbm, up, 3)

    row = lax.broadcasted_iota(jnp.int32, (SUB, SUB), 0)
    col = lax.broadcasted_iota(jnp.int32, (SUB, SUB), 1)
    hnat[...] = (1 - 2 * parity(jnp.bitwise_and(row, col))).astype(F32).astype(BF16)
    hperm[...] = (1 - 2 * parity(jnp.bitwise_and(natural(row), col))).astype(F32).astype(BF16)
    eye[...] = (row == col).astype(F32).astype(BF16)
    pick[...] = (natural(row) == col).astype(F32).astype(BF16)

    def dequant(codes, scales, weights, m, base):
        for g in range(2):
            words = codes[base + g * HALF:base + (g + 1) * HALF, :]
            low, high = centred_pair(words)
            scale = scales[2 * m + g:2 * m + g + 1, :]
            weights[m, g * HALF:(g + 1) * HALF, :] = (low * scale).astype(BF16)
            weights[m, WORDS + g * HALF:WORDS + (g + 1) * HALF, :] = (high * scale).astype(BF16)

    def p_copy(b):
        rows = pl.ds(pl.multiple_of((1 - core) * TH, TH), TH)
        return remote(pbuf.at[b, rows], prx.at[b], p_s, p_r.at[b], partner)

    def x_copy(b, k):
        rows = pl.ds(pl.multiple_of(lax.rem(x + k, NX) * TS, TS), TS)
        return remote(sbuf.at[b, rows], xrx.at[b, k - 1], x_s, x_r.at[b], x_dev(k))

    def y_copy(b, k):
        return remote(rg.at[0, b], rg.at[k, b], y_s, y_r, y_dev(k))

    def f_copy(k):
        return remote(hd.at[0], hd.at[k], f_s, f_r, y_dev(k))

    def first_product(b):
        if b:
            dc_copy(b).wait()
        dequant(dc, ds, dw, b, b * WORDS)
        pbuf[b] = lax.dot_general(og[...], dw[b], NT, preferred_element_type=F32).astype(BF16)

    def pair_sum(b):
        p_copy(b).wait_recv()
        own = pbuf[b, pl.ds(pl.multiple_of(core * TH, TH), TH), :].astype(F32)
        sbuf[b] = (own + prx[b].astype(F32)).astype(BF16)
        for k in [far] + near:
            x_copy(b, k).start()

    loads["ds"].wait()
    loads["og"].wait()
    dc_copy(0).wait()
    first_product(0)
    load("gs", gs_hbm, gs, 4)
    load("us", us_hbm, us, 5)
    load("gc", gc_hbm, gc, 7)
    load("uc", uc_hbm, uc, 8)
    load("inp", inp_hbm, inp, 6)
    pl.semaphore_wait(barrier, len(peers))
    p_copy(0).start()

    loads["gp"].wait()
    loads["up"].wait()
    gate = gp[my_rows, :].astype(F32)
    hidden = (gate * (1.0 / (1.0 + jnp.exp(-gate))) * up[my_rows, :].astype(F32)).astype(BF16)
    for b in range(NB):
        hd[0, b] = hidden[:, b * SUB:(b + 1) * SUB]
    for k in range(1, NY):
        f_copy(k).start()

    for b in range(1, NB):
        first_product(b)
        p_copy(b).start()
        if b >= 2:
            pair_sum(b - 2)
    pair_sum(NB - 2)
    pair_sum(NB - 1)

    @pl.loop(0, T // 32)
    def _(i):
        rows = pl.ds(pl.multiple_of(i * 32, 32), 32)
        g = gp[rows, :].astype(F32)
        sg = 1.0 / (1.0 + jnp.exp(-g))
        act[rows, :] = g * sg
        slope[rows, :] = up[rows, :].astype(F32) * (sg * (1.0 + g * (1.0 - sg)))

    def sign_of(k):
        source = lax.rem(y + NY - k, NY)
        both = jnp.bitwise_and(source, y)
        odd = jnp.bitwise_and(jnp.bitwise_xor(both, jnp.right_shift(both, 1)), 1)
        return (1 - 2 * odd).astype(F32)

    def rotate(parts, signs):
        turned = jnp.dot(
            parts[...].reshape(NY * NB * TS, SUB), signs[...], preferred_element_type=F32
        ).reshape(NY, NB, TS, SUB)
        total = turned[0] * sign_of(0)
        for k in range(1, NY):
            total = total + turned[k] * sign_of(k)
        pieces = [total[b] for b in range(NB)]
        step = 1
        while step < NB:
            fresh = list(pieces)
            for b in range(NB):
                if b & step:
                    fresh[b] = pieces[b - step] - pieces[b]
                else:
                    fresh[b] = pieces[b] + pieces[b + step]
            pieces = fresh
            step = step * 2
        return jnp.concatenate(pieces, axis=1) * (HB ** -0.5)

    def spread_x(buf, ssem, rsem, k):
        return remote(buf.at[mine], buf.at[mine], ssem, rsem, x_dev(k))

    def slot_from(k):
        return core * NX + lax.rem(x + NX - k, NX)

    def slot_of_partner(k):
        return (1 - core) * NX + lax.rem(x + NX - k, NX)

    def spread_pair(buf, ssem, rsem, k):
        slot = slot_from(k)
        return remote(buf.at[slot], buf.at[slot], ssem, rsem, partner)

    def spread(buf, xs, xr, ps, pr):
        for k in near:
            spread_x(buf, xs, xr(k), k).start()
        spread_pair(buf, ps, pr(0), 0).start()

    loads["gs"].wait()
    loads["us"].wait()
    loads["gc"].wait()

    def turn(weights, turned, m):
        for f in range(F // SUB):
            block = weights[m, :, f * SUB:(f + 1) * SUB]
            across = lax.dot_general(eye[...], block, NT, preferred_element_type=F32)
            turned[f * SUB:(f + 1) * SUB, m * SUB:(m + 1) * SUB] = across.astype(BF16)

    def prepare(codes, scales, weights, turned):
        for m in range(NM):
            dequant(codes, scales, weights, m, m * WORDS)
            if m:
                turn(weights, turned, m - 1)
        turn(weights, turned, NM - 1)

    prepare(gc, gs, gw, gwt)

    for b in range(NB):
        total = sbuf[b, pl.ds(pl.multiple_of(x * TS, TS), TS), :].astype(F32)
        all_of(xrx.at[b], x_r.at[b])
        for k in range(1, NX):
            total = total + xrx[b, k - 1].astype(F32)
        rg[0, b] = total.astype(BF16)
        for k in [2, 1, 3]:
            y_copy(b, k).start()

    def flip(block):
        return lax.dot_general(pick[...], block, NT, preferred_element_type=F32).astype(BF16)

    def group_sums(codes, left, right, scales, out, j, count):
        cols = pl.ds(pl.multiple_of(j * SUB, SUB), SUB)
        for m in range(count):
            full = jnp.dot(left[m], right[:, cols], preferred_element_type=F32)
            low, high = centred_pair(codes[m * WORDS:(m + 1) * WORDS, cols])
            prod = full[:WORDS] * low + full[WORDS:] * high
            for g in range(2):
                line = jnp.sum(prod[g * HALF:(g + 1) * HALF], axis=0, keepdims=True)
                out[2 * m + g:2 * m + g + 1, cols] = line * scales[2 * m + g:2 * m + g + 1, cols]

    all_of(hd.at[pl.ds(1, NY - 1)], f_r)
    rta[mine] = rotate(hd, hnat).astype(BF16)
    spread(rta, ra_s, lambda k: ra_r, rp_s, lambda k: rp_r)
    spread_x(rta, ra_s, ra_r, far).start()

    loads["uc"].wait()
    prepare(uc, us, uw, uwt)

    all_of(rg.at[pl.ds(1, NY - 1)], y_r)
    hga[mine] = rotate(rg, hperm).astype(BF16)
    spread(hga, ga_s, lambda k: ga_r.at[k - 1], gp_s, lambda k: gp_r.at[k])

    def part_cols(part, parts):
        return pl.ds(part * D // parts, D // parts)

    def ry_copy(slot, cols, sem, k):
        return remote(
            ybuf.at[slot, lax.rem(y + k, NY), :, cols], yrx.at[slot, k - 1, :, cols],
            ry_s, ry_r.at[sem], y_dev(k),
        )

    def rz_copy(k, cols):
        return remote(
            zbuf.at[lax.rem(z + k, NZ), :, cols], zrx.at[k - 1, :, cols], rz_s, rz_r, z_dev(k)
        )

    def slot_rows(slot):
        return pl.ds(pl.multiple_of(slot * TS, TS), TS)

    def factors(slots):
        for slot in slots:
            rows = slot_rows(slot)
            hg = hga[slot].astype(F32)
            gg[rows, :] = (hg * slope[rows, :]).astype(BF16)
            ug[rows, :] = (hg * act[rows, :]).astype(BF16)

    def products(slots, part, parts, sem):
        for m in range(part * NM // parts, (part + 1) * NM // parts):
            left = jnp.concatenate([gg[slot_rows(slot), :] for slot in slots], axis=0)
            both = jnp.dot(left, gwt[:, m * SUB:(m + 1) * SUB], preferred_element_type=F32)
            left = jnp.concatenate([ug[slot_rows(slot), :] for slot in slots], axis=0)
            both = both + jnp.dot(left, uwt[:, m * SUB:(m + 1) * SUB], preferred_element_type=F32)
            for i, slot in enumerate(slots):
                piece = both[i * TS:(i + 1) * TS].reshape(NY, 8, SUB).astype(BF16)
                ybuf[slot, :, :, m * SUB:(m + 1) * SUB] = piece
        for slot in slots:
            for k in [2, 1, 3]:
                ry_copy(slot, part_cols(part, parts), sem, k).start()

    def y_sums(slots, part, parts, sem):
        cols = part_cols(part, parts)
        all_of(yrx.at[pl.ds(0, len(slots)), :, :, cols], ry_r.at[sem])
        for slot in slots:
            total = ybuf[slot, y, :, cols].astype(F32)
            for k in range(1, NY):
                total = total + yrx[slot, k - 1, :, cols].astype(F32)
            zbuf[slot, :, cols] = total.astype(BF16)

            @pl.when(slot != z)
            def _():
                rz_copy(lax.rem(slot - z + NZ, NZ), cols).start()

    def from_x(k):
        spread_x(hga, ga_s, ga_r.at[k - 1], k).wait_recv()
        spread_pair(hga, gp_s, gp_r.at[k], k).start()

    def from_pair(k):
        slot = slot_of_partner(k)
        remote(hga.at[slot], hga.at[slot], gp_s, gp_r.at[k], partner).wait_recv()


    loads["inp"].wait()
    for m in range(NM):
        xt[m] = flip(inp[:, m * SUB:(m + 1) * SUB])
    first = [mine, slot_of_partner(0)]
    second = [slot_from(k) for k in near]
    third = [slot_of_partner(k) for k in near]
    fourth = [slot_from(far), slot_of_partner(far)]
    from_pair(0)
    spread_x(hga, ga_s, ga_r.at[far - 1], far).start()
    factors(first)
    products(first, 0, 2, 0)
    products(first, 1, 2, 0)
    all_of(rta.at[pl.ds(0, NX - 1)], ra_r)
    for k in range(1, NX):
        spread_pair(rta, rp_s, rp_r, k).start()
    for k in near:
        from_x(k)
    if near:
        factors(second)
        for part in range(2):
            products(second, part, 2, 1)
    for k in near:
        from_pair(k)
    if near:
        factors(third)
        products(third, 0, 2, 2)
    from_x(far)
    if near:
        products(third, 1, 2, 2)
    y_sums(first, 0, 1, 0)
    from_pair(far)
    factors(fourth)
    for part in range(2):
        products(fourth, part, 2, 3 + part)

    all_of(rta.at[pl.ds(0, NX)], rp_r)
    whole = rta[...].reshape(T, F)
    for b in range(NB):
        rt[b] = flip(whole[:, b * SUB:(b + 1) * SUB])

    def sums_over(*args):
        def run(start, stop):
            @pl.loop(start, stop)
            def _(j):
                group_sums(*args[:5], j, args[5])

        return run

    down_sums = sums_over(dc, rt, og, ds, dl_out, NB)
    gate_sums = sums_over(gc, xt, gg, gs, gl_out, NM)
    up_sums = sums_over(uc, xt, ug, us, ul_out, NM)
    blocks = F // SUB

    if near:
        y_sums(second, 0, 1, 1)
    down_sums(0, NM)
    if near:
        y_sums(third, 0, 1, 2)
    gate_sums(0, blocks // 2)
    y_sums(fourth, 0, 2, 3)
    gate_sums(blocks // 2, blocks)
    y_sums(fourth, 1, 2, 4)
    up_sums(0, blocks)

    total = zbuf[z].astype(F32)
    all_of(zrx, rz_r)
    for k in range(1, NZ):
        total = total + zrx[k - 1].astype(F32)
    for m in range(NM):
        unpick[m] = total[:, m * SUB:(m + 1) * SUB]
    ordered = jnp.dot(
        unpick[...].reshape(NM * 8, SUB).astype(BF16), pick[...], preferred_element_type=F32
    ).astype(BF16).astype(F32).reshape(NM, 8, SUB)
    for m in range(NM):
        gi_out[:, m * SUB:(m + 1) * SUB] = ordered[m].astype(BF16)

    all_of(prx, p_s)
    all_of(xrx, x_s)
    all_of(rg.at[pl.ds(1, NY - 1)], y_s)
    all_of(hd.at[pl.ds(1, NY - 1)], f_s)
    all_of(rta.at[pl.ds(0, NX - 1)], ra_s)
    all_of(hga.at[pl.ds(0, NX - 1)], ga_s)
    all_of(rta.at[pl.ds(0, NX)], rp_s)
    all_of(hga.at[pl.ds(0, NX)], gp_s)
    all_of(yrx, ry_s)
    all_of(zrx, rz_s)


def hand_out(*refs):
    sem = refs[8]
    copies = [pltpu.make_async_copy(refs[i], refs[4 + i], sem.at[i]) for i in range(4)]
    for copy in copies:
        copy.start()
    for copy in copies:
        copy.wait()


def shards(hid, wid, inputs, gate_pre, up_pre, out_grad, gate_codes, up_codes, down_codes, gate_scale, up_scale, down_scale):
    T, D = inputs.shape
    F = gate_pre.shape[1]
    NY = HB // F
    NZ = hid // NY
    NX = wid // 2
    NB, NM = F // SUB, D // SUB
    TS, TH = T // wid, T // 2
    V = pltpu.VMEM
    dma = lambda *shape: pltpu.SemaphoreType.DMA(shape)
    one = pltpu.SemaphoreType.DMA
    scratch = [
        V((T, D), BF16), V((T, F), BF16), V((T, F), BF16), V((T, D), BF16),
        V((D // 2, F), jnp.int32), V((D // 2, F), jnp.int32), V((F // 2, D), jnp.int32),
        V(gate_scale.shape, F32), V(up_scale.shape, F32), V(down_scale.shape, F32),
        V((NM, SUB, F), BF16), V((NM, SUB, F), BF16), V((NB, SUB, D), BF16), V((F, D), BF16), V((F, D), BF16),
        V((T, F), F32), V((T, F), F32),
        V((NM, SUB, T), BF16), V((NB, SUB, T), BF16),
        V((T, F), BF16), V((T, F), BF16),
        V((SUB, SUB), BF16), V((SUB, SUB), BF16), V((SUB, SUB), BF16), V((SUB, SUB), BF16), V((NM, 8, SUB), F32),
        V((NB, T, SUB), BF16), V((NB, TH, SUB), BF16), V((NB, TH, SUB), BF16),
        V((NB, NX - 1, TS, SUB), BF16),
        V((NY, NB, TS, SUB), BF16), V((NY, NB, TS, SUB), BF16),
        V((wid, TS, F), BF16), V((wid, TS, F), BF16),
        V((wid, NY, 8, D), BF16), V((wid, NY - 1, 8, D), BF16),
        V((NZ, 8, D), BF16), V((NZ - 1, 8, D), BF16),
        dma(9), dma(NB),
        one, dma(NB), one, dma(NB), one, one, one, one,
        one, dma(NX - 1), one, dma(NX), one, one, one, one,
        one, dma(5), one, one,
    ]
    results = pl.pallas_call(
        functools.partial(body, (NX, NY, NZ, T, D, F)),
        out_shape=(
            V((T // hid, D), BF16), V(gate_scale.shape, F32), V(up_scale.shape, F32), V(down_scale.shape, F32),
        ),
        in_specs=[pl.BlockSpec(memory_space=pl.ANY)] * 10,
        out_specs=[pl.BlockSpec(memory_space=pltpu.VMEM)] * 4,
        scratch_shapes=scratch,
        compiler_params=pltpu.CompilerParams(
            collective_id=0, has_side_effects=True, vmem_limit_bytes=60 * 1024 * 1024
        ),
        name="layer",
    )(inputs, gate_pre, up_pre, out_grad, gate_codes, up_codes, down_codes, gate_scale, up_scale, down_scale)
    return pl.pallas_call(
        hand_out,
        out_shape=[jax.ShapeDtypeStruct(r.shape, r.dtype) for r in results],
        in_specs=[pl.BlockSpec(memory_space=pltpu.VMEM)] * 4,
        out_specs=[pl.BlockSpec(memory_space=pl.ANY)] * 4,
        scratch_shapes=[dma(4)],
        name="hand_out",
    )(*[pltpu.with_memory_space_constraint(r, pltpu.VMEM) for r in results])


def solution(mesh):
    in_specs = (
        P(None, "wid"),
        P(None, "hid"),
        P(None, "hid"),
        P(None, "wid"),
        P("wid", "hid"),
        P("wid", "hid"),
        P("hid", "wid"),
        P("wid", "hid"),
        P("wid", "hid"),
        P("hid", "wid"),
    )
    out_specs = (P("hid", "wid"), P("wid", "hid"), P("wid", "hid"), P("hid", "wid"))
    fn = functools.partial(shards, mesh.shape["hid"], mesh.shape["wid"])
    return jax.shard_map(fn, mesh=mesh, in_specs=in_specs, out_specs=out_specs, check_vma=False)
```

```python
import functools
import jax
import jax.numpy as jnp
from jax import lax
from jax.experimental import pallas as pl
from jax.experimental.pallas import tpu as pltpu
from jax.sharding import PartitionSpec as P

HB = 4096
GROUP = 128
SUB = 256
WORDS = SUB // 2
HALF = GROUP // 2
F32 = jnp.float32
BF16 = jnp.bfloat16
NT = (((1,), (1,)), ((), ()))


def parity(v):
    v = jnp.bitwise_xor(v, jnp.right_shift(v, 4))
    v = jnp.bitwise_xor(v, jnp.right_shift(v, 2))
    v = jnp.bitwise_xor(v, jnp.right_shift(v, 1))
    return jnp.bitwise_and(v, 1)


def natural(k):
    return 2 * jnp.bitwise_and(k, WORDS - 1) + jnp.right_shift(k, 7)


def centred_pair(words):
    low = (jnp.bitwise_and(words, 15) - 8).astype(F32)
    high = (jnp.right_shift(words, 4) - 8).astype(F32)
    return low, high


def body(
    dims,
    inp_hbm, gp_hbm, up_hbm, og_hbm, gc_hbm, uc_hbm, dc_hbm, gs_hbm, us_hbm, ds_hbm,
    gi_out, gl_out, ul_out, dl_out,
    inp, gp, up, og, gc, uc, dc, gs, us, ds,
    gw, uw, dw, gwt, uwt, act, slope, xt, rt, gg, ug,
    hnat, hperm, pick, eye, unpick,
    pbuf, prx, sbuf, xrx, rg, hd, hga, rta, ybuf, yrx, zbuf, zrx,
    plane_in, line_in, load_sem, dc_sem,
    p_s, p_r, x_s, x_r, y_s, y_r, f_s, f_r, ga_s, ga_r, gp_s, gp_r, ra_s, ra_r, rp_s, rp_r,
    ry_s, ry_r, rz_s, rz_r,
):
    NX, NY, NZ, T, D, F = dims
    NB = F // SUB
    NM = D // SUB
    TS = T // (2 * NX)
    TH = T // 2
    h = lax.axis_index("hid")
    w = lax.axis_index("wid")
    x = w // 2
    core = w % 2
    z = h // NY
    y = h % NY
    mine = core * NX + x

    def x_dev(k):
        return (h, lax.rem(x + k, NX) * 2 + core)

    def y_dev(k):
        return (z * NY + lax.rem(y + k, NY), w)

    def z_dev(k):
        return (lax.rem(z + k, NZ) * NY + y, w)

    partner = (h, x * 2 + 1 - core)
    near = [1, NX - 1] if NX > 2 else []
    far = NX // 2

    def remote(src, dst, ssem, rsem, dev):
        return pltpu.make_async_remote_copy(
            src_ref=src, dst_ref=dst, send_sem=ssem, recv_sem=rsem,
            device_id=dev, device_id_type=pl.DeviceIdType.MESH,
        )

    def all_of(ref, sem):
        pltpu.make_async_copy(ref, ref, sem).wait()

    barrier = pltpu.get_barrier_semaphore()
    def tell(sem, dev):
        pl.semaphore_signal(sem, inc=1, device_id=dev, device_id_type=pl.DeviceIdType.MESH)

    tell(barrier, partner)
    for k in range(1, NX):
        tell(barrier, (h, lax.rem(x + k, NX) * 2))
    for k in range(1, NY):
        tell(barrier, (z * NY + lax.rem(y + k, NY), 2 * x))
    for k in range(1, NZ):
        tell(barrier, (lax.rem(z + k, NZ) * NY + y, 2 * x + 1))

    my_rows = pl.ds(pl.multiple_of(mine * TS, TS), TS)
    loads = {}

    def load(name, src, dst, idx):
        copy = pltpu.make_async_copy(src, dst, load_sem.at[idx])
        copy.start()
        loads[name] = copy

    def dc_copy(b):
        rows = pl.ds(pl.multiple_of(b * WORDS, WORDS), WORDS)
        return pltpu.make_async_copy(dc_hbm.at[rows], dc.at[rows], dc_sem.at[b])

    load("ds", ds_hbm, ds, 0)
    dc_copy(0).start()
    load("og", og_hbm, og, 1)
    for b in range(1, NB):
        dc_copy(b).start()
    load("gp", gp_hbm, gp, 2)
    load("up", up_hbm, up, 3)

    row = lax.broadcasted_iota(jnp.int32, (SUB, SUB), 0)
    col = lax.broadcasted_iota(jnp.int32, (SUB, SUB), 1)
    hnat[...] = (1 - 2 * parity(jnp.bitwise_and(row, col))).astype(F32).astype(BF16)
    hperm[...] = (1 - 2 * parity(jnp.bitwise_and(natural(row), col))).astype(F32).astype(BF16)
    eye[...] = (row == col).astype(F32).astype(BF16)
    pick[...] = (natural(row) == col).astype(F32).astype(BF16)

    def dequant(codes, scales, weights, m, base):
        for g in range(2):
            words = codes[base + g * HALF:base + (g + 1) * HALF, :]
            low, high = centred_pair(words)
            scale = scales[2 * m + g:2 * m + g + 1, :]
            weights[m, g * HALF:(g + 1) * HALF, :] = (low * scale).astype(BF16)
            weights[m, WORDS + g * HALF:WORDS + (g + 1) * HALF, :] = (high * scale).astype(BF16)

    def p_copy(b):
        rows = pl.ds(pl.multiple_of((1 - core) * TH, TH), TH)
        return remote(pbuf.at[b, rows], prx.at[b], p_s, p_r.at[b], partner)

    def x_copy(b, k):
        rows = pl.ds(pl.multiple_of(lax.rem(x + k, NX) * TS, TS), TS)
        return remote(sbuf.at[b, rows], xrx.at[b, k - 1], x_s, x_r.at[b], x_dev(k))

    def y_copy(b, k):
        return remote(rg.at[0, b], rg.at[k, b], y_s, y_r, y_dev(k))

    def f_copy(k):
        return remote(hd.at[0], hd.at[k], f_s, f_r, y_dev(k))

    def first_product(b):
        if b:
            dc_copy(b).wait()
        dequant(dc, ds, dw, b, b * WORDS)
        pbuf[b] = lax.dot_general(og[...], dw[b], NT, preferred_element_type=F32).astype(BF16)

    def pair_sum(b):
        p_copy(b).wait_recv()
        own = pbuf[b, pl.ds(pl.multiple_of(core * TH, TH), TH), :].astype(F32)
        sbuf[b] = (own + prx[b].astype(F32)).astype(BF16)
        for k in [far] + near:
            x_copy(b, k).start()

    loads["ds"].wait()
    loads["og"].wait()
    dc_copy(0).wait()
    first_product(0)
    load("gs", gs_hbm, gs, 4)
    load("us", us_hbm, us, 5)
    load("gc", gc_hbm, gc, 7)
    load("uc", uc_hbm, uc, 8)
    load("inp", inp_hbm, inp, 6)
    @pl.when(core == 0)
    def _():
        pl.semaphore_wait(barrier, 2 * (NX + NY - 2) + 1)
        tell(plane_in, partner)

    @pl.when(core == 1)
    def _():
        pl.semaphore_wait(plane_in, 1)

    p_copy(0).start()

    loads["gp"].wait()
    loads["up"].wait()
    gate = gp[my_rows, :].astype(F32)
    hidden = (gate * (1.0 / (1.0 + jnp.exp(-gate))) * up[my_rows, :].astype(F32)).astype(BF16)
    for b in range(NB):
        hd[0, b] = hidden[:, b * SUB:(b + 1) * SUB]
    for k in range(1, NY):
        f_copy(k).start()

    for b in range(1, NB):
        first_product(b)
        p_copy(b).start()
        if b >= 2:
            pair_sum(b - 2)
    pair_sum(NB - 2)
    pair_sum(NB - 1)

    @pl.loop(0, T // 32)
    def _(i):
        rows = pl.ds(pl.multiple_of(i * 32, 32), 32)
        g = gp[rows, :].astype(F32)
        sg = 1.0 / (1.0 + jnp.exp(-g))
        act[rows, :] = g * sg
        slope[rows, :] = up[rows, :].astype(F32) * (sg * (1.0 + g * (1.0 - sg)))

    def sign_of(k):
        source = lax.rem(y + NY - k, NY)
        both = jnp.bitwise_and(source, y)
        odd = jnp.bitwise_and(jnp.bitwise_xor(both, jnp.right_shift(both, 1)), 1)
        return (1 - 2 * odd).astype(F32)

    def rotate(parts, signs):
        turned = jnp.dot(
            parts[...].reshape(NY * NB * TS, SUB), signs[...], preferred_element_type=F32
        ).reshape(NY, NB, TS, SUB)
        total = turned[0] * sign_of(0)
        for k in range(1, NY):
            total = total + turned[k] * sign_of(k)
        pieces = [total[b] for b in range(NB)]
        step = 1
        while step < NB:
            fresh = list(pieces)
            for b in range(NB):
                if b & step:
                    fresh[b] = pieces[b - step] - pieces[b]
                else:
                    fresh[b] = pieces[b] + pieces[b + step]
            pieces = fresh
            step = step * 2
        return jnp.concatenate(pieces, axis=1) * (HB ** -0.5)

    def spread_x(buf, ssem, rsem, k):
        return remote(buf.at[mine], buf.at[mine], ssem, rsem, x_dev(k))

    def slot_from(k):
        return core * NX + lax.rem(x + NX - k, NX)

    def slot_of_partner(k):
        return (1 - core) * NX + lax.rem(x + NX - k, NX)

    def spread_pair(buf, ssem, rsem, k):
        slot = slot_from(k)
        return remote(buf.at[slot], buf.at[slot], ssem, rsem, partner)

    def spread(buf, xs, xr, ps, pr):
        for k in near:
            spread_x(buf, xs, xr(k), k).start()
        spread_pair(buf, ps, pr(0), 0).start()

    loads["gs"].wait()
    loads["us"].wait()
    loads["gc"].wait()

    def turn(weights, turned, m):
        for f in range(F // SUB):
            block = weights[m, :, f * SUB:(f + 1) * SUB]
            across = lax.dot_general(eye[...], block, NT, preferred_element_type=F32)
            turned[f * SUB:(f + 1) * SUB, m * SUB:(m + 1) * SUB] = across.astype(BF16)

    def prepare(codes, scales, weights, turned):
        for m in range(NM):
            dequant(codes, scales, weights, m, m * WORDS)
            if m:
                turn(weights, turned, m - 1)
        turn(weights, turned, NM - 1)

    prepare(gc, gs, gw, gwt)

    for b in range(NB):
        total = sbuf[b, pl.ds(pl.multiple_of(x * TS, TS), TS), :].astype(F32)
        all_of(xrx.at[b], x_r.at[b])
        for k in range(1, NX):
            total = total + xrx[b, k - 1].astype(F32)
        rg[0, b] = total.astype(BF16)
        for k in [2, 1, 3]:
            y_copy(b, k).start()

    def flip(block):
        return lax.dot_general(pick[...], block, NT, preferred_element_type=F32).astype(BF16)

    def group_sums(codes, left, right, scales, out, j, count):
        cols = pl.ds(pl.multiple_of(j * SUB, SUB), SUB)
        for m in range(count):
            full = jnp.dot(left[m], right[:, cols], preferred_element_type=F32)
            low, high = centred_pair(codes[m * WORDS:(m + 1) * WORDS, cols])
            prod = full[:WORDS] * low + full[WORDS:] * high
            for g in range(2):
                line = jnp.sum(prod[g * HALF:(g + 1) * HALF], axis=0, keepdims=True)
                out[2 * m + g:2 * m + g + 1, cols] = line * scales[2 * m + g:2 * m + g + 1, cols]

    all_of(hd.at[pl.ds(1, NY - 1)], f_r)
    rta[mine] = rotate(hd, hnat).astype(BF16)
    spread(rta, ra_s, lambda k: ra_r, rp_s, lambda k: rp_r)
    spread_x(rta, ra_s, ra_r, far).start()

    loads["uc"].wait()
    prepare(uc, us, uw, uwt)

    all_of(rg.at[pl.ds(1, NY - 1)], y_r)
    hga[mine] = rotate(rg, hperm).astype(BF16)
    spread(hga, ga_s, lambda k: ga_r.at[k - 1], gp_s, lambda k: gp_r.at[k])

    def part_cols(part, parts):
        return pl.ds(part * D // parts, D // parts)

    def ry_copy(slot, cols, sem, k):
        return remote(
            ybuf.at[slot, lax.rem(y + k, NY), :, cols], yrx.at[slot, k - 1, :, cols],
            ry_s, ry_r.at[sem], y_dev(k),
        )

    def rz_copy(k, cols):
        return remote(
            zbuf.at[lax.rem(z + k, NZ), :, cols], zrx.at[k - 1, :, cols], rz_s, rz_r, z_dev(k)
        )

    def slot_rows(slot):
        return pl.ds(pl.multiple_of(slot * TS, TS), TS)

    def factors(slots):
        for slot in slots:
            rows = slot_rows(slot)
            hg = hga[slot].astype(F32)
            gg[rows, :] = (hg * slope[rows, :]).astype(BF16)
            ug[rows, :] = (hg * act[rows, :]).astype(BF16)

    def products(slots, part, parts):
        for m in range(part * NM // parts, (part + 1) * NM // parts):
            left = jnp.concatenate([gg[slot_rows(slot), :] for slot in slots], axis=0)
            both = jnp.dot(left, gwt[:, m * SUB:(m + 1) * SUB], preferred_element_type=F32)
            left = jnp.concatenate([ug[slot_rows(slot), :] for slot in slots], axis=0)
            both = both + jnp.dot(left, uwt[:, m * SUB:(m + 1) * SUB], preferred_element_type=F32)
            for i, slot in enumerate(slots):
                piece = both[i * TS:(i + 1) * TS].reshape(NY, 8, SUB).astype(BF16)
                ybuf[slot, :, :, m * SUB:(m + 1) * SUB] = piece

    def send(slots, part, parts, sem):
        for slot in slots:
            for k in [2, 1, 3]:
                ry_copy(slot, part_cols(part, parts), sem, k).start()

    def y_sums(slots, part, parts, sem):
        cols = part_cols(part, parts)
        all_of(yrx.at[pl.ds(0, len(slots)), :, :, cols], ry_r.at[sem])
        for slot in slots:
            total = ybuf[slot, y, :, cols].astype(F32)
            for k in range(1, NY):
                total = total + yrx[slot, k - 1, :, cols].astype(F32)
            zbuf[slot, :, cols] = total.astype(BF16)

            @pl.when(slot != z)
            def _():
                rz_copy(lax.rem(slot - z + NZ, NZ), cols).start()

    def from_x(k):
        spread_x(hga, ga_s, ga_r.at[k - 1], k).wait_recv()
        spread_pair(hga, gp_s, gp_r.at[k], k).start()

    def from_pair(k):
        slot = slot_of_partner(k)
        remote(hga.at[slot], hga.at[slot], gp_s, gp_r.at[k], partner).wait_recv()


    loads["inp"].wait()
    for m in range(NM):
        xt[m] = flip(inp[:, m * SUB:(m + 1) * SUB])
    first = [mine, slot_of_partner(0)]
    second = [slot_from(k) for k in near]
    def pick_slot(on_first, on_second):
        return on_first + core * (on_second - on_first)

    if near:
        third = [
            pick_slot(slot_from(far), slot_of_partner(near[0])),
            pick_slot(slot_of_partner(near[0]), slot_of_partner(near[1])),
        ]
        fourth = [
            pick_slot(slot_of_partner(near[1]), slot_of_partner(far)),
            pick_slot(slot_of_partner(far), slot_from(far)),
        ]
    else:
        third = []
        fourth = [pick_slot(slot_from(far), slot_of_partner(far)), pick_slot(slot_of_partner(far), slot_from(far))]
    from_pair(0)
    spread_x(hga, ga_s, ga_r.at[far - 1], far).start()
    factors(first)
    for part in range(2):
        products(first, part, 2)
        send(first, part, 2, 0)
    all_of(rta.at[pl.ds(0, NX - 1)], ra_r)
    for k in range(1, NX):
        spread_pair(rta, rp_s, rp_r, k).start()
    for k in near:
        from_x(k)
    if near:
        factors(second)
        for part in range(2):
            products(second, part, 2)

            @pl.when(core == 0)
            def _():
                send(second, part, 2, 1)
    for k in near:
        from_pair(k)
    from_x(far)
    if near:
        factors(third)
        for part in range(2):
            products(third, part, 2)
            send(third, part, 2, 2)
    @pl.when(core == 1)
    def _():
        pl.semaphore_wait(barrier, 2 * (NZ - 1) + 1)
        tell(line_in, partner)

    @pl.when(core == 0)
    def _():
        pl.semaphore_wait(line_in, 1)

    y_sums(first, 0, 1, 0)
    from_pair(far)
    factors(fourth)
    for part in range(2):
        products(fourth, part, 2)
        send(fourth, part, 2, 3 + part)
    if near:
        @pl.when(core == 1)
        def _():
            for part in range(2):
                send(second, part, 2, 1)

    if near:
        @pl.when(core == 0)
        def _():
            y_sums(second, 0, 1, 1)

    all_of(rta.at[pl.ds(0, NX)], rp_r)
    whole = rta[...].reshape(T, F)
    for b in range(NB):
        rt[b] = flip(whole[:, b * SUB:(b + 1) * SUB])

    def sums_over(*args):
        def run(start, stop):
            @pl.loop(start, stop)
            def _(j):
                group_sums(*args[:5], j, args[5])

        return run

    down_sums = sums_over(dc, rt, og, ds, dl_out, NB)
    gate_sums = sums_over(gc, xt, gg, gs, gl_out, NM)
    up_sums = sums_over(uc, xt, ug, us, ul_out, NM)
    blocks = F // SUB

    down_sums(0, 2 * NM // 3)
    if near:
        y_sums(third, 0, 1, 2)
    down_sums(2 * NM // 3, NM)
    y_sums(fourth, 0, 2, 3)
    y_sums(fourth, 1, 2, 4)
    if near:
        @pl.when(core == 1)
        def _():
            y_sums(second, 0, 1, 1)
    gate_sums(0, blocks)
    up_sums(0, blocks)

    total = zbuf[z].astype(F32)
    all_of(zrx, rz_r)
    for k in range(1, NZ):
        total = total + zrx[k - 1].astype(F32)
    for m in range(NM):
        unpick[m] = total[:, m * SUB:(m + 1) * SUB]
    ordered = jnp.dot(
        unpick[...].reshape(NM * 8, SUB).astype(BF16), pick[...], preferred_element_type=F32
    ).astype(BF16).astype(F32).reshape(NM, 8, SUB)
    for m in range(NM):
        gi_out[:, m * SUB:(m + 1) * SUB] = ordered[m].astype(BF16)

    all_of(prx, p_s)
    all_of(xrx, x_s)
    all_of(rg.at[pl.ds(1, NY - 1)], y_s)
    all_of(hd.at[pl.ds(1, NY - 1)], f_s)
    all_of(rta.at[pl.ds(0, NX - 1)], ra_s)
    all_of(hga.at[pl.ds(0, NX - 1)], ga_s)
    all_of(rta.at[pl.ds(0, NX)], rp_s)
    all_of(hga.at[pl.ds(0, NX)], gp_s)
    all_of(yrx, ry_s)
    all_of(zrx, rz_s)


def hand_out(*refs):
    sem = refs[8]
    copies = [pltpu.make_async_copy(refs[i], refs[4 + i], sem.at[i]) for i in range(4)]
    for copy in copies:
        copy.start()
    for copy in copies:
        copy.wait()


def shards(hid, wid, inputs, gate_pre, up_pre, out_grad, gate_codes, up_codes, down_codes, gate_scale, up_scale, down_scale):
    T, D = inputs.shape
    F = gate_pre.shape[1]
    NY = HB // F
    NZ = hid // NY
    NX = wid // 2
    NB, NM = F // SUB, D // SUB
    TS, TH = T // wid, T // 2
    V = pltpu.VMEM
    dma = lambda *shape: pltpu.SemaphoreType.DMA(shape)
    one = pltpu.SemaphoreType.DMA
    scratch = [
        V((T, D), BF16), V((T, F), BF16), V((T, F), BF16), V((T, D), BF16),
        V((D // 2, F), jnp.int32), V((D // 2, F), jnp.int32), V((F // 2, D), jnp.int32),
        V(gate_scale.shape, F32), V(up_scale.shape, F32), V(down_scale.shape, F32),
        V((NM, SUB, F), BF16), V((NM, SUB, F), BF16), V((NB, SUB, D), BF16), V((F, D), BF16), V((F, D), BF16),
        V((T, F), F32), V((T, F), F32),
        V((NM, SUB, T), BF16), V((NB, SUB, T), BF16),
        V((T, F), BF16), V((T, F), BF16),
        V((SUB, SUB), BF16), V((SUB, SUB), BF16), V((SUB, SUB), BF16), V((SUB, SUB), BF16), V((NM, 8, SUB), F32),
        V((NB, T, SUB), BF16), V((NB, TH, SUB), BF16), V((NB, TH, SUB), BF16),
        V((NB, NX - 1, TS, SUB), BF16),
        V((NY, NB, TS, SUB), BF16), V((NY, NB, TS, SUB), BF16),
        V((wid, TS, F), BF16), V((wid, TS, F), BF16),
        V((wid, NY, 8, D), BF16), V((wid, NY - 1, 8, D), BF16),
        V((NZ, 8, D), BF16), V((NZ - 1, 8, D), BF16),
        pltpu.SemaphoreType.REGULAR, pltpu.SemaphoreType.REGULAR, dma(9), dma(NB),
        one, dma(NB), one, dma(NB), one, one, one, one,
        one, dma(NX - 1), one, dma(NX), one, one, one, one,
        one, dma(5), one, one,
    ]
    results = pl.pallas_call(
        functools.partial(body, (NX, NY, NZ, T, D, F)),
        out_shape=(
            V((T // hid, D), BF16), V(gate_scale.shape, F32), V(up_scale.shape, F32), V(down_scale.shape, F32),
        ),
        in_specs=[pl.BlockSpec(memory_space=pl.ANY)] * 10,
        out_specs=[pl.BlockSpec(memory_space=pltpu.VMEM)] * 4,
        scratch_shapes=scratch,
        compiler_params=pltpu.CompilerParams(
            collective_id=0, has_side_effects=True, vmem_limit_bytes=60 * 1024 * 1024
        ),
        name="layer",
    )(inputs, gate_pre, up_pre, out_grad, gate_codes, up_codes, down_codes, gate_scale, up_scale, down_scale)
    return pl.pallas_call(
        hand_out,
        out_shape=[jax.ShapeDtypeStruct(r.shape, r.dtype) for r in results],
        in_specs=[pl.BlockSpec(memory_space=pltpu.VMEM)] * 4,
        out_specs=[pl.BlockSpec(memory_space=pl.ANY)] * 4,
        scratch_shapes=[dma(4)],
        name="hand_out",
    )(*[pltpu.with_memory_space_constraint(r, pltpu.VMEM) for r in results])


def solution(mesh):
    in_specs = (
        P(None, "wid"),
        P(None, "hid"),
        P(None, "hid"),
        P(None, "wid"),
        P("wid", "hid"),
        P("wid", "hid"),
        P("hid", "wid"),
        P("wid", "hid"),
        P("wid", "hid"),
        P("hid", "wid"),
    )
    out_specs = (P("hid", "wid"), P("wid", "hid"), P("wid", "hid"), P("hid", "wid"))
    fn = functools.partial(shards, mesh.shape["hid"], mesh.shape["wid"])
    return jax.shard_map(fn, mesh=mesh, in_specs=in_specs, out_specs=out_specs, check_vma=False)
```

```python
import functools
import jax
import jax.numpy as jnp
from jax import lax
from jax.experimental import pallas as pl
from jax.experimental.pallas import tpu as pltpu
from jax.sharding import PartitionSpec as P

HB = 4096
GROUP = 128
SUB = 256
WORDS = SUB // 2
HALF = GROUP // 2
F32 = jnp.float32
BF16 = jnp.bfloat16
NT = (((1,), (1,)), ((), ()))


def parity(v):
    v = jnp.bitwise_xor(v, jnp.right_shift(v, 4))
    v = jnp.bitwise_xor(v, jnp.right_shift(v, 2))
    v = jnp.bitwise_xor(v, jnp.right_shift(v, 1))
    return jnp.bitwise_and(v, 1)


def natural(k):
    return 2 * jnp.bitwise_and(k, WORDS - 1) + jnp.right_shift(k, 7)


def centred_pair(words):
    low = (jnp.bitwise_and(words, 15) - 8).astype(F32)
    high = (jnp.right_shift(words, 4) - 8).astype(F32)
    return low, high


def body(
    dims,
    inp_hbm, gp_hbm, up_hbm, og_hbm, gc_hbm, uc_hbm, dc_hbm, gs_hbm, us_hbm, ds_hbm,
    gi_out, gl_out, ul_out, dl_out,
    inp, gp, up, og, gc, uc, dc, gs, us, ds,
    gw, uw, dw, gwt, uwt, act, slope, xt, rt, gg, ug,
    hnat, hperm, pick, eye, unpick,
    pbuf, prx, sbuf, xrx, rg, hd, hga, rta, ybuf, yrx, zbuf, zrx,
    plane_in, line_in, load_sem, dc_sem,
    p_s, p_r, x_s, x_r, y_s, y_r, f_s, f_r, ga_s, ga_r, gp_s, gp_r, ra_s, ra_r, rp_s, rp_r,
    ry_s, ry_r, rz_s, rz_r,
):
    NX, NY, NZ, T, D, F = dims
    NB = F // SUB
    NM = D // SUB
    TS = T // (2 * NX)
    TH = T // 2
    h = lax.axis_index("hid")
    w = lax.axis_index("wid")
    x = w // 2
    core = w % 2
    z = h // NY
    y = h % NY
    mine = core * NX + x

    def x_dev(k):
        return (h, lax.rem(x + k, NX) * 2 + core)

    def y_dev(k):
        return (z * NY + lax.rem(y + k, NY), w)

    def z_dev(k):
        return (lax.rem(z + k, NZ) * NY + y, w)

    partner = (h, x * 2 + 1 - core)
    near = [1, NX - 1] if NX > 2 else []
    far = NX // 2

    def remote(src, dst, ssem, rsem, dev):
        return pltpu.make_async_remote_copy(
            src_ref=src, dst_ref=dst, send_sem=ssem, recv_sem=rsem,
            device_id=dev, device_id_type=pl.DeviceIdType.MESH,
        )

    def all_of(ref, sem):
        pltpu.make_async_copy(ref, ref, sem).wait()

    barrier = pltpu.get_barrier_semaphore()
    def tell(sem, dev):
        pl.semaphore_signal(sem, inc=1, device_id=dev, device_id_type=pl.DeviceIdType.MESH)

    tell(barrier, partner)
    for k in range(1, NX):
        tell(barrier, (h, lax.rem(x + k, NX) * 2))
    for k in range(1, NY):
        tell(barrier, (z * NY + lax.rem(y + k, NY), 2 * x))
    for k in range(1, NZ):
        tell(barrier, (lax.rem(z + k, NZ) * NY + y, 2 * x + 1))

    my_rows = pl.ds(pl.multiple_of(mine * TS, TS), TS)
    loads = {}

    def load(name, src, dst, idx):
        copy = pltpu.make_async_copy(src, dst, load_sem.at[idx])
        copy.start()
        loads[name] = copy

    def dc_copy(b):
        rows = pl.ds(pl.multiple_of(b * WORDS, WORDS), WORDS)
        return pltpu.make_async_copy(dc_hbm.at[rows], dc.at[rows], dc_sem.at[b])

    load("ds", ds_hbm, ds, 0)
    dc_copy(0).start()
    load("og", og_hbm, og, 1)
    for b in range(1, NB):
        dc_copy(b).start()
    load("gp", gp_hbm, gp, 2)
    load("up", up_hbm, up, 3)

    row = lax.broadcasted_iota(jnp.int32, (SUB, SUB), 0)
    col = lax.broadcasted_iota(jnp.int32, (SUB, SUB), 1)
    hnat[...] = (1 - 2 * parity(jnp.bitwise_and(row, col))).astype(F32).astype(BF16)
    hperm[...] = (1 - 2 * parity(jnp.bitwise_and(natural(row), col))).astype(F32).astype(BF16)
    eye[...] = (row == col).astype(F32).astype(BF16)
    pick[...] = (natural(row) == col).astype(F32).astype(BF16)

    def dequant(codes, scales, weights, m, base):
        for g in range(2):
            words = codes[base + g * HALF:base + (g + 1) * HALF, :]
            low, high = centred_pair(words)
            scale = scales[2 * m + g:2 * m + g + 1, :]
            weights[m, g * HALF:(g + 1) * HALF, :] = (low * scale).astype(BF16)
            weights[m, WORDS + g * HALF:WORDS + (g + 1) * HALF, :] = (high * scale).astype(BF16)

    def p_copy(b):
        rows = pl.ds(pl.multiple_of((1 - core) * TH, TH), TH)
        return remote(pbuf.at[b, rows], prx.at[b], p_s, p_r.at[b], partner)

    def x_copy(b, k):
        rows = pl.ds(pl.multiple_of(lax.rem(x + k, NX) * TS, TS), TS)
        return remote(sbuf.at[b, rows], xrx.at[b, k - 1], x_s, x_r.at[b], x_dev(k))

    def y_copy(b, k):
        return remote(rg.at[0, b], rg.at[k, b], y_s, y_r, y_dev(k))

    def f_copy(k):
        return remote(hd.at[0], hd.at[k], f_s, f_r, y_dev(k))

    def first_product(b):
        if b:
            dc_copy(b).wait()
        dequant(dc, ds, dw, b, b * WORDS)
        pbuf[b] = lax.dot_general(og[...], dw[b], NT, preferred_element_type=F32).astype(BF16)

    def pair_sum(b):
        p_copy(b).wait_recv()
        own = pbuf[b, pl.ds(pl.multiple_of(core * TH, TH), TH), :].astype(F32)
        sbuf[b] = (own + prx[b].astype(F32)).astype(BF16)
        for k in [far] + near:
            x_copy(b, k).start()

    loads["ds"].wait()
    loads["og"].wait()
    dc_copy(0).wait()
    first_product(0)
    load("gs", gs_hbm, gs, 4)
    load("us", us_hbm, us, 5)
    load("gc", gc_hbm, gc, 7)
    load("uc", uc_hbm, uc, 8)
    load("inp", inp_hbm, inp, 6)
    @pl.when(core == 0)
    def _():
        pl.semaphore_wait(barrier, 2 * (NX + NY - 2) + 1)
        tell(plane_in, partner)

    @pl.when(core == 1)
    def _():
        pl.semaphore_wait(plane_in, 1)

    p_copy(0).start()

    loads["gp"].wait()
    loads["up"].wait()
    gate = gp[my_rows, :].astype(F32)
    hidden = (gate * (1.0 / (1.0 + jnp.exp(-gate))) * up[my_rows, :].astype(F32)).astype(BF16)
    for b in range(NB):
        hd[0, b] = hidden[:, b * SUB:(b + 1) * SUB]
    for k in range(1, NY):
        f_copy(k).start()

    for b in range(1, NB):
        first_product(b)
        p_copy(b).start()
        if b >= 2:
            pair_sum(b - 2)
    pair_sum(NB - 2)
    pair_sum(NB - 1)

    @pl.loop(0, T // 32)
    def _(i):
        rows = pl.ds(pl.multiple_of(i * 32, 32), 32)
        g = gp[rows, :].astype(F32)
        sg = 1.0 / (1.0 + jnp.exp(-g))
        act[rows, :] = g * sg
        slope[rows, :] = up[rows, :].astype(F32) * (sg * (1.0 + g * (1.0 - sg)))

    def sign_of(k):
        source = lax.rem(y + NY - k, NY)
        both = jnp.bitwise_and(source, y)
        odd = jnp.bitwise_and(jnp.bitwise_xor(both, jnp.right_shift(both, 1)), 1)
        return (1 - 2 * odd).astype(F32)

    def rotate(parts, signs):
        turned = jnp.dot(
            parts[...].reshape(NY * NB * TS, SUB), signs[...], preferred_element_type=F32
        ).reshape(NY, NB, TS, SUB)
        total = turned[0] * sign_of(0)
        for k in range(1, NY):
            total = total + turned[k] * sign_of(k)
        pieces = [total[b] for b in range(NB)]
        step = 1
        while step < NB:
            fresh = list(pieces)
            for b in range(NB):
                if b & step:
                    fresh[b] = pieces[b - step] - pieces[b]
                else:
                    fresh[b] = pieces[b] + pieces[b + step]
            pieces = fresh
            step = step * 2
        return jnp.concatenate(pieces, axis=1) * (HB ** -0.5)

    def spread_x(buf, ssem, rsem, k):
        return remote(buf.at[mine], buf.at[mine], ssem, rsem, x_dev(k))

    def slot_from(k):
        return core * NX + lax.rem(x + NX - k, NX)

    def slot_of_partner(k):
        return (1 - core) * NX + lax.rem(x + NX - k, NX)

    def spread_pair(buf, ssem, rsem, k):
        slot = slot_from(k)
        return remote(buf.at[slot], buf.at[slot], ssem, rsem, partner)

    def spread(buf, xs, xr, ps, pr):
        for k in near:
            spread_x(buf, xs, xr(k), k).start()
        spread_pair(buf, ps, pr(0), 0).start()

    loads["gs"].wait()
    loads["us"].wait()
    loads["gc"].wait()

    def turn(weights, turned, m):
        for f in range(F // SUB):
            block = weights[m, :, f * SUB:(f + 1) * SUB]
            across = lax.dot_general(eye[...], block, NT, preferred_element_type=F32)
            turned[f * SUB:(f + 1) * SUB, m * SUB:(m + 1) * SUB] = across.astype(BF16)

    def prepare(codes, scales, weights, turned):
        for m in range(NM):
            dequant(codes, scales, weights, m, m * WORDS)
            if m:
                turn(weights, turned, m - 1)
        turn(weights, turned, NM - 1)

    prepare(gc, gs, gw, gwt)

    for b in range(NB):
        total = sbuf[b, pl.ds(pl.multiple_of(x * TS, TS), TS), :].astype(F32)
        all_of(xrx.at[b], x_r.at[b])
        for k in range(1, NX):
            total = total + xrx[b, k - 1].astype(F32)
        rg[0, b] = total.astype(BF16)
        for k in [2, 1, 3]:
            y_copy(b, k).start()

    def flip(block):
        return lax.dot_general(pick[...], block, NT, preferred_element_type=F32).astype(BF16)

    def group_sums(codes, left, right, scales, out, j, count):
        cols = pl.ds(pl.multiple_of(j * SUB, SUB), SUB)
        for m in range(count):
            full = jnp.dot(left[m], right[:, cols], preferred_element_type=F32)
            low, high = centred_pair(codes[m * WORDS:(m + 1) * WORDS, cols])
            prod = full[:WORDS] * low + full[WORDS:] * high
            for g in range(2):
                line = jnp.sum(prod[g * HALF:(g + 1) * HALF], axis=0, keepdims=True)
                out[2 * m + g:2 * m + g + 1, cols] = line * scales[2 * m + g:2 * m + g + 1, cols]

    all_of(hd.at[pl.ds(1, NY - 1)], f_r)
    rta[mine] = rotate(hd, hnat).astype(BF16)
    spread(rta, ra_s, lambda k: ra_r, rp_s, lambda k: rp_r)
    spread_x(rta, ra_s, ra_r, far).start()

    loads["uc"].wait()
    prepare(uc, us, uw, uwt)

    all_of(rg.at[pl.ds(1, NY - 1)], y_r)
    hga[mine] = rotate(rg, hperm).astype(BF16)
    spread(hga, ga_s, lambda k: ga_r.at[k - 1], gp_s, lambda k: gp_r.at[k])

    def part_cols(part, parts):
        return pl.ds(pl.multiple_of(part * (D // parts), SUB), D // parts)

    def ry_copy(slot, cols, sem, k):
        return remote(
            ybuf.at[slot, lax.rem(y + k, NY), :, cols], yrx.at[slot, k - 1, :, cols],
            ry_s, ry_r.at[sem], y_dev(k),
        )

    def rz_copy(k, cols):
        return remote(
            zbuf.at[lax.rem(z + k, NZ), :, cols], zrx.at[k - 1, :, cols], rz_s, rz_r, z_dev(k)
        )

    def slot_rows(slot):
        return pl.ds(pl.multiple_of(slot * TS, TS), TS)

    def factors(slots):
        for slot in slots:
            rows = slot_rows(slot)
            hg = hga[slot].astype(F32)
            gg[rows, :] = (hg * slope[rows, :]).astype(BF16)
            ug[rows, :] = (hg * act[rows, :]).astype(BF16)

    def products(slots, part, parts):
        for n in range(NM // parts):
            m = part * (NM // parts) + n
            cols = pl.ds(pl.multiple_of(m * SUB, SUB), SUB)
            left = jnp.concatenate([gg[slot_rows(slot), :] for slot in slots], axis=0)
            both = jnp.dot(left, gwt[:, cols], preferred_element_type=F32)
            left = jnp.concatenate([ug[slot_rows(slot), :] for slot in slots], axis=0)
            both = both + jnp.dot(left, uwt[:, cols], preferred_element_type=F32)
            for i, slot in enumerate(slots):
                piece = both[i * TS:(i + 1) * TS].reshape(NY, 8, SUB).astype(BF16)
                ybuf[slot, :, :, cols] = piece

    def send(slots, part, parts, sem):
        for slot in slots:
            for k in [2, 1, 3]:
                ry_copy(slot, part_cols(part, parts), sem, k).start()

    def y_sums(slots, part, parts, sem):
        cols = part_cols(part, parts)
        all_of(yrx.at[pl.ds(0, len(slots)), :, :, cols], ry_r.at[sem])
        for slot in slots:
            total = ybuf[slot, y, :, cols].astype(F32)
            for k in range(1, NY):
                total = total + yrx[slot, k - 1, :, cols].astype(F32)
            zbuf[slot, :, cols] = total.astype(BF16)

            @pl.when(slot != z)
            def _():
                rz_copy(lax.rem(slot - z + NZ, NZ), cols).start()

    def from_x(k):
        spread_x(hga, ga_s, ga_r.at[k - 1], k).wait_recv()
        spread_pair(hga, gp_s, gp_r.at[k], k).start()

    def from_pair(k):
        slot = slot_of_partner(k)
        remote(hga.at[slot], hga.at[slot], gp_s, gp_r.at[k], partner).wait_recv()


    loads["inp"].wait()
    for m in range(NM):
        xt[m] = flip(inp[:, m * SUB:(m + 1) * SUB])
    first = [mine, slot_of_partner(0)]
    second = [slot_from(k) for k in near]
    def pick_slot(on_first, on_second):
        return on_first + core * (on_second - on_first)

    if near:
        third = [
            pick_slot(slot_from(far), slot_of_partner(near[0])),
            pick_slot(slot_of_partner(near[0]), slot_of_partner(near[1])),
        ]
        fourth = [
            pick_slot(slot_of_partner(near[1]), slot_of_partner(far)),
            pick_slot(slot_of_partner(far), slot_from(far)),
        ]
    else:
        third = []
        fourth = [pick_slot(slot_from(far), slot_of_partner(far)), pick_slot(slot_of_partner(far), slot_from(far))]
    from_pair(0)
    spread_x(hga, ga_s, ga_r.at[far - 1], far).start()
    factors(first)
    @pl.loop(0, 2)
    def _(part):
        products(first, part, 2)
        send(first, part, 2, 0)
    all_of(rta.at[pl.ds(0, NX - 1)], ra_r)
    for k in range(1, NX):
        spread_pair(rta, rp_s, rp_r, k).start()
    for k in near:
        from_x(k)
    if near:
        factors(second)
        @pl.loop(0, 2)
        def _(part):
            products(second, part, 2)

            @pl.when(core == 0)
            def _():
                send(second, part, 2, 1)
    for k in near:
        from_pair(k)
    from_x(far)
    if near:
        factors(third)
        @pl.loop(0, 2)
        def _(part):
            products(third, part, 2)
            send(third, part, 2, 2)
    @pl.when(core == 1)
    def _():
        pl.semaphore_wait(barrier, 2 * (NZ - 1) + 1)
        tell(line_in, partner)

    @pl.when(core == 0)
    def _():
        pl.semaphore_wait(line_in, 1)

    y_sums(first, 0, 1, 0)
    from_pair(far)
    factors(fourth)
    @pl.loop(0, 2)
    def _(part):
        products(fourth, part, 2)
        send(fourth, part, 2, 3 + part)
    if near:
        @pl.when(core == 1)
        def _():
            for part in range(2):
                send(second, part, 2, 1)

    if near:
        @pl.when(core == 0)
        def _():
            y_sums(second, 0, 1, 1)

    all_of(rta.at[pl.ds(0, NX)], rp_r)
    whole = rta[...].reshape(T, F)
    for b in range(NB):
        rt[b] = flip(whole[:, b * SUB:(b + 1) * SUB])

    def sums_over(*args):
        def run(start, stop):
            @pl.loop(start, stop)
            def _(j):
                group_sums(*args[:5], j, args[5])

        return run

    down_sums = sums_over(dc, rt, og, ds, dl_out, NB)
    gate_sums = sums_over(gc, xt, gg, gs, gl_out, NM)
    up_sums = sums_over(uc, xt, ug, us, ul_out, NM)
    blocks = F // SUB

    down_sums(0, 2 * NM // 3)
    if near:
        y_sums(third, 0, 1, 2)
    down_sums(2 * NM // 3, NM)
    y_sums(fourth, 0, 2, 3)
    y_sums(fourth, 1, 2, 4)
    if near:
        @pl.when(core == 1)
        def _():
            y_sums(second, 0, 1, 1)
    gate_sums(0, blocks)
    up_sums(0, blocks)

    total = zbuf[z].astype(F32)
    all_of(zrx, rz_r)
    for k in range(1, NZ):
        total = total + zrx[k - 1].astype(F32)
    for m in range(NM):
        unpick[m] = total[:, m * SUB:(m + 1) * SUB]
    ordered = jnp.dot(
        unpick[...].reshape(NM * 8, SUB).astype(BF16), pick[...], preferred_element_type=F32
    ).astype(BF16).astype(F32).reshape(NM, 8, SUB)
    for m in range(NM):
        gi_out[:, m * SUB:(m + 1) * SUB] = ordered[m].astype(BF16)

    all_of(prx, p_s)
    all_of(xrx, x_s)
    all_of(rg.at[pl.ds(1, NY - 1)], y_s)
    all_of(hd.at[pl.ds(1, NY - 1)], f_s)
    all_of(rta.at[pl.ds(0, NX - 1)], ra_s)
    all_of(hga.at[pl.ds(0, NX - 1)], ga_s)
    all_of(rta.at[pl.ds(0, NX)], rp_s)
    all_of(hga.at[pl.ds(0, NX)], gp_s)
    all_of(yrx, ry_s)
    all_of(zrx, rz_s)


def hand_out(*refs):
    sem = refs[8]
    copies = [pltpu.make_async_copy(refs[i], refs[4 + i], sem.at[i]) for i in range(4)]
    for copy in copies:
        copy.start()
    for copy in copies:
        copy.wait()


def shards(hid, wid, inputs, gate_pre, up_pre, out_grad, gate_codes, up_codes, down_codes, gate_scale, up_scale, down_scale):
    T, D = inputs.shape
    F = gate_pre.shape[1]
    NY = HB // F
    NZ = hid // NY
    NX = wid // 2
    NB, NM = F // SUB, D // SUB
    TS, TH = T // wid, T // 2
    V = pltpu.VMEM
    dma = lambda *shape: pltpu.SemaphoreType.DMA(shape)
    one = pltpu.SemaphoreType.DMA
    scratch = [
        V((T, D), BF16), V((T, F), BF16), V((T, F), BF16), V((T, D), BF16),
        V((D // 2, F), jnp.int32), V((D // 2, F), jnp.int32), V((F // 2, D), jnp.int32),
        V(gate_scale.shape, F32), V(up_scale.shape, F32), V(down_scale.shape, F32),
        V((NM, SUB, F), BF16), V((NM, SUB, F), BF16), V((NB, SUB, D), BF16), V((F, D), BF16), V((F, D), BF16),
        V((T, F), F32), V((T, F), F32),
        V((NM, SUB, T), BF16), V((NB, SUB, T), BF16),
        V((T, F), BF16), V((T, F), BF16),
        V((SUB, SUB), BF16), V((SUB, SUB), BF16), V((SUB, SUB), BF16), V((SUB, SUB), BF16), V((NM, 8, SUB), F32),
        V((NB, T, SUB), BF16), V((NB, TH, SUB), BF16), V((NB, TH, SUB), BF16),
        V((NB, NX - 1, TS, SUB), BF16),
        V((NY, NB, TS, SUB), BF16), V((NY, NB, TS, SUB), BF16),
        V((wid, TS, F), BF16), V((wid, TS, F), BF16),
        V((wid, NY, 8, D), BF16), V((wid, NY - 1, 8, D), BF16),
        V((NZ, 8, D), BF16), V((NZ - 1, 8, D), BF16),
        pltpu.SemaphoreType.REGULAR, pltpu.SemaphoreType.REGULAR, dma(9), dma(NB),
        one, dma(NB), one, dma(NB), one, one, one, one,
        one, dma(NX - 1), one, dma(NX), one, one, one, one,
        one, dma(5), one, one,
    ]
    results = pl.pallas_call(
        functools.partial(body, (NX, NY, NZ, T, D, F)),
        out_shape=(
            V((T // hid, D), BF16), V(gate_scale.shape, F32), V(up_scale.shape, F32), V(down_scale.shape, F32),
        ),
        in_specs=[pl.BlockSpec(memory_space=pl.ANY)] * 10,
        out_specs=[pl.BlockSpec(memory_space=pltpu.VMEM)] * 4,
        scratch_shapes=scratch,
        compiler_params=pltpu.CompilerParams(
            collective_id=0, has_side_effects=True, vmem_limit_bytes=60 * 1024 * 1024
        ),
        name="layer",
    )(inputs, gate_pre, up_pre, out_grad, gate_codes, up_codes, down_codes, gate_scale, up_scale, down_scale)
    return pl.pallas_call(
        hand_out,
        out_shape=[jax.ShapeDtypeStruct(r.shape, r.dtype) for r in results],
        in_specs=[pl.BlockSpec(memory_space=pltpu.VMEM)] * 4,
        out_specs=[pl.BlockSpec(memory_space=pl.ANY)] * 4,
        scratch_shapes=[dma(4)],
        name="hand_out",
    )(*[pltpu.with_memory_space_constraint(r, pltpu.VMEM) for r in results])


def solution(mesh):
    in_specs = (
        P(None, "wid"),
        P(None, "hid"),
        P(None, "hid"),
        P(None, "wid"),
        P("wid", "hid"),
        P("wid", "hid"),
        P("hid", "wid"),
        P("wid", "hid"),
        P("wid", "hid"),
        P("hid", "wid"),
    )
    out_specs = (P("hid", "wid"), P("wid", "hid"), P("wid", "hid"), P("hid", "wid"))
    fn = functools.partial(shards, mesh.shape["hid"], mesh.shape["wid"])
    return jax.shard_map(fn, mesh=mesh, in_specs=in_specs, out_specs=out_specs, check_vma=False)
```
